128 devices in a mesh: grp: 4 (over z_lo, core), tp: 32 (over z_hi, x, y).
Axes of the slice: x: 4, y: 4, z: 4 (z_hi: 2, z_lo: 2; z = z_hi * 2 + z_lo), core: 2. Of those that a mesh axis runs over, the one named last changes fastest.
Arguments:
- teacher_hidden: bfloat16 [384, 8192], P(('grp', 'tp')), may hold values from -150 to 150
- teacher_head: bfloat16 [8192, 98304], P(None, ('grp', 'tp')), may hold values from -0.0625 to 0.0625
- student_hidden: bfloat16 [384, 3584], P(('grp', 'tp')), may hold values from -150 to 150
- student_head: bfloat16 [3584, 98304], P(None, ('grp', 'tp')), may hold values from -0.09375 to 0.09375
- labels: int32 [384], replicated, may hold values from 0 to 98303
- owner_map: int32 [384], replicated, may hold values from 0 to 383, each once
Outputs:
- token_loss: float32 [384], P(('grp', 'tp'))
- grad_head: bfloat16 [3584, 98304], P(None, ('grp', 'tp'))
- grad_hidden: bfloat16 [384, 3584], P(('grp', 'tp'))
The draws below stay inside these ranges and needn't reach their ends.
Inputs may be any that keep to these rules, and one draw needn't show every extreme that they name: owner_map holds each of 0 to 383 once.
All inputs are finite; a program needn't handle non-finite values.
Results may differ from the reference program's by a relative error of at most 0.0085.
Values may be sent and summed in bfloat16 or wider, within the bound.
No kernel may reach another device: no remote copies, remote signals or barrier semaphores. Data moves between devices by JAX's collectives and lax.ppermute only.
A program may use at most 128 MiB of HBM per device.

```python
import math
import jax
import jax.numpy as jnp
import numpy as np
from jax import lax

TEACHER_DIM = 8192
STUDENT_DIM = 3584
VOCABULARY = 98304
TOKENS = 384


def rough_rows(key, rows, cols):
    first, second = jax.random.split(key)
    values = jnp.clip(jax.random.normal(first, (rows, cols), jnp.float32), -4.0, 4.0)
    scales = jnp.exp(jax.random.uniform(second, (rows, 1), jnp.float32, math.log(1.5), math.log(6.0)))
    return values * scales


def draw_teacher_hidden(key, part):
    inner = jax.random.fold_in(key, 17)
    return rough_rows(inner, TOKENS, TEACHER_DIM).astype(jnp.bfloat16)


def draw_student_hidden(key, part):
    inner = jax.random.fold_in(key, 29)
    return rough_rows(inner, TOKENS, STUDENT_DIM).astype(jnp.bfloat16)


def with_ends(result, rng, least, largest):
    spot = [jax.random.randint(jax.random.fold_in(rng, axis), (), 0, length) for axis, length in enumerate(result.shape)]
    longest = result.shape.index(max(result.shape))
    beside = spot[:longest] + [(spot[longest] + 1) % result.shape[longest]] + spot[longest + 1:]
    return result.at[tuple(spot)].set(least).at[tuple(beside)].set(largest)


def steps_of(rng, shape, cuts, low, high):
    factor_of = 1.0
    for axis_at, shards_of in cuts:
        draws = jax.random.uniform(jax.random.fold_in(jax.random.fold_in(rng, 6), axis_at), (shards_of,), jnp.float32, low / len(cuts), high / len(cuts))
        factor_of = factor_of * jnp.repeat(jnp.exp(draws), shape[axis_at] // shards_of).reshape((-1,) + (1,) * (len(shape) - 1 - axis_at))
    return factor_of


def skewed_wide(stream_key, dims, amount, lean):
    loads = [min(1 << octave, amount + 1 - (1 << octave)) * (1 << 20) // math.isqrt((1 << octave) ** lean) + 1 for octave in range((amount + 1).bit_length()) if 1 << octave <= amount]
    width = 1 + sum(loads) // (1 << 30)
    table = np.cumsum(np.array([max(1, weight // width) for weight in loads]))
    pick = jax.random.randint(jax.random.fold_in(stream_key, 1), dims, 0, int(table[len(loads) - 1]))
    start = jnp.left_shift(1, jnp.searchsorted(jnp.asarray(table, jnp.int32), pick, side="right").astype(jnp.int32))
    grade = start - 1 + jax.random.randint(jax.random.fold_in(stream_key, 4), dims, 0, 1 << 30) % jnp.minimum(start, amount + 1 - start)
    return jax.random.permutation(jax.random.fold_in(stream_key, 2), amount)[grade].astype(jnp.int32)


def gaussian(own_key, shape, scale, limit, cuts=(), dtype=jnp.bfloat16):
    array = scale * jax.random.normal(own_key, shape, jnp.float32)
    if cuts:
        array = array * steps_of(own_key, shape, cuts, -0.22, 0.18)
    return jnp.clip(array, -limit, limit).astype(dtype)


def setup_inputs(seed: int = 0) -> dict:
    seeds = jax.random.split(jax.random.key(seed), 7)
    return {
        "teacher_hidden": draw_teacher_hidden(jax.random.fold_in(seeds[6], 71), 0),
        "teacher_head": gaussian(seeds[1], (TEACHER_DIM, VOCABULARY), TEACHER_DIM ** -0.5, 0.0625, ((1, 128),)),
        "student_hidden": draw_student_hidden(jax.random.fold_in(seeds[6], 71), 0),
        "student_head": gaussian(seeds[3], (STUDENT_DIM, VOCABULARY), STUDENT_DIM ** -0.5, 0.09375, ((1, 128),)),
        "labels": with_ends(skewed_wide(seeds[4], (TOKENS,), VOCABULARY, 2), jax.random.fold_in(seeds[4], 3), 0, VOCABULARY - 1).astype(jnp.int32),
        "owner_map": jax.random.permutation(seeds[5], TOKENS).astype(jnp.int32),
    }


def row_terms(teacher_rows, student_rows, teacher_lse, student_lse, weight, reverse, hits):
    log_teacher = teacher_rows - teacher_lse[:, None]
    log_student = student_rows - student_lse[:, None]
    teacher_prob = jnp.exp(log_teacher)
    student_prob = jnp.exp(log_student)
    mixed = weight[:, None] * (student_prob - teacher_prob)
    mixed = mixed + (1.0 - weight)[:, None] * student_prob * (log_student - log_teacher - reverse[:, None])
    mixed = mixed + student_prob - hits.astype(jnp.float32)
    return (mixed / TOKENS).astype(jnp.bfloat16)


def whole_rows(teacher_rows, student_rows, hits):
    teacher_top = jnp.max(teacher_rows, axis=1)
    student_top = jnp.max(student_rows, axis=1)
    teacher_lse = teacher_top + jnp.log(jnp.sum(jnp.exp(teacher_rows - teacher_top[:, None]), axis=1))
    student_lse = student_top + jnp.log(jnp.sum(jnp.exp(student_rows - student_top[:, None]), axis=1))
    log_teacher = teacher_rows - teacher_lse[:, None]
    log_student = student_rows - student_lse[:, None]
    teacher_prob = jnp.exp(log_teacher)
    student_prob = jnp.exp(log_student)
    entropy = -jnp.sum(teacher_prob * log_teacher, axis=1)
    weight = entropy / math.log(VOCABULARY)
    forward = jnp.sum(teacher_prob * (log_teacher - log_student), axis=1)
    reverse = jnp.sum(student_prob * (log_student - log_teacher), axis=1)
    cross = student_lse - jnp.sum(jnp.where(hits, student_rows, 0.0), axis=1)
    loss = weight * forward + (1.0 - weight) * reverse + cross
    return loss, row_terms(teacher_rows, student_rows, teacher_lse, student_lse, weight, reverse, hits)


def reference(teacher_hidden, teacher_head, student_hidden, student_head, labels, owner_map):
    ordered = jnp.take(teacher_hidden, owner_map, axis=0)
    teacher_logits = jnp.dot(ordered, teacher_head, preferred_element_type=jnp.float32)
    student_logits = jnp.dot(student_hidden, student_head, preferred_element_type=jnp.float32)
    hits = labels[:, None] == lax.iota(jnp.int32, VOCABULARY)[None, :]
    token_loss, grad_logits = whole_rows(teacher_logits, student_logits, hits)
    grad_head = jnp.dot(student_hidden.T, grad_logits, preferred_element_type=jnp.float32).astype(jnp.bfloat16)
    grad_hidden = jnp.dot(grad_logits, student_head.T, preferred_element_type=jnp.float32).astype(jnp.bfloat16)
    return (token_loss, grad_head, grad_hidden)
```

```python
import functools
import math

import jax
import jax.numpy as jnp
from jax import lax
from jax.experimental import pallas as pl
from jax.experimental.pallas import tpu as pltpu
from jax.sharding import PartitionSpec as P

AXES = ("grp", "tp")
DEVICES = 128
TOKENS = 384
ROWS = 3
BF16 = jnp.bfloat16
F32 = jnp.float32
VMEM = pl.BlockSpec(memory_space=pltpu.VMEM)
SMEM = pl.BlockSpec(memory_space=pltpu.SMEM)
ANY = pl.BlockSpec(memory_space=pl.ANY)
STAGES = (("y", "x", "z"), ("y", "z", "x"))


def coords(d):
    return {"zl": d // 64, "c": d // 32 % 2, "zh": d // 16 % 2, "x": d // 4 % 4, "y": d % 4, "z": d // 16 % 2 * 2 + d // 64}


def device(c, x, y, z):
    return ((z % 2 * 2 + c) * 2 + z // 2) * 16 + x * 4 + y


def moved(d, dim, k):
    at = coords(d)
    at[dim] = (at[dim] + k) % 4
    return device(at["c"], at["x"], at["y"], at["z"])


def swap(value):
    return lax.ppermute(value, AXES, [(d, d ^ 32) for d in range(DEVICES)])


def shift(value, stage, k):
    pairs = [(d, moved(d, STAGES[coords(d)["c"]][stage], k)) for d in range(DEVICES)]
    return lax.ppermute(value, AXES, pairs)


def shift_dim(value, dim, k):
    return lax.ppermute(value, AXES, [(d, moved(d, dim, k)) for d in range(DEVICES)])


def token_order(me, half):
    j = lax.iota(jnp.int32, TOKENS)
    steps = (j // 6 % 4, j // 24 % 4, j // 96)
    at = {dim: (me[dim] - step) % 4 for dim, step in zip(STAGES[half], steps)}
    core = (half + j % 6 // ROWS) % 2
    return device(core, at["x"], at["y"], at["z"]) * ROWS + j % ROWS


def split3(v):
    high = v.astype(BF16)
    rest = v - high.astype(F32)
    middle = rest.astype(BF16)
    return high, middle, (rest - middle.astype(F32)).astype(BF16)


def one_hot(column, row):
    return jnp.where(column == row, 1.0, 0.0).astype(BF16)


def dot(a, b):
    return jnp.dot(a, b, preferred_element_type=F32)


def dot_nt(a, b):
    return lax.dot_general(a, b, (((1,), (1,)), ((), ())), preferred_element_type=F32)


def pick_column(column, row_ids, row_values):
    return jnp.sum(jnp.where(column == row_ids, row_values.astype(F32), 0.0), axis=1, keepdims=True)


def logits_kernel(dims, last, *refs):
    tk, sk, tstep, sstep = dims
    refs = list(refs)
    at_ref, g0, g1, g2, g3, tok_half, tok_col, owner, labels, tw, sw = refs[:11]
    refs = refs[11:]
    if last:
        t_in, s_in = refs[:2]
        refs = refs[2:]
        t_out, s_out, h_out, stats_out = refs[:4]
        refs = refs[4:]
    else:
        t_out, s_out, h_out = refs[:3]
        refs = refs[3:]
    g, tbuf, sbuf, tsem, ssem = refs
    half = at_ref[0]
    tn, sn = tk // tstep, sk // sstep
    copies = []
    for i in range(tn):
        rows = pl.ds(pl.multiple_of(half * tk + i * tstep, tstep), tstep)
        copies.append(pltpu.make_async_copy(tw.at[rows, :], tbuf.at[pl.ds(i * tstep, tstep), :], tsem.at[i]))
    for i in range(sn):
        rows = pl.ds(pl.multiple_of(half * sk + i * sstep, sstep), sstep)
        copies.append(pltpu.make_async_copy(sw.at[rows, :], sbuf.at[pl.ds(i * sstep, sstep), :], ssem.at[i]))
    for copy in copies:
        copy.start()
    for k, block in enumerate((g0, g1, g2, g3)):
        g[pl.ds(96 * k, 96), :] = block[...]
    lanes = lax.broadcasted_iota(jnp.int32, (1, TOKENS), 1)
    owner_col = pick_column(tok_col[...], lanes, owner[...])
    pick_t = one_hot(owner_col, tok_half[...].astype(F32))
    pick_s = one_hot(tok_col[...], tok_half[...])
    if last:
        t_out[...] = t_in[...]
        s_out[...] = s_in[...]
    for i in range(tn):
        a = dot(pick_t, g[:, pl.ds(i * tstep, tstep)]).astype(BF16)
        copies[i].wait()
        part = dot(a, tbuf[pl.ds(i * tstep, tstep), :])
        if i == 0 and not last:
            t_out[...] = part
        else:
            t_out[...] += part
    for i in range(sn):
        a = dot(pick_s, g[:, pl.ds(tk + i * sstep, sstep)]).astype(BF16)
        h_out[:, pl.ds(i * sstep, sstep)] = a
        copies[tn + i].wait()
        part = dot(a, sbuf[pl.ds(i * sstep, sstep), :])
        if i == 0 and not last:
            s_out[...] = part
        else:
            s_out[...] += part
    if not last:
        return
    base = at_ref[1]
    label_col = pick_column(tok_col[...], lanes, labels[...]).astype(jnp.int32) - base
    step = 64
    lane = lax.broadcasted_iota(jnp.int32, (step, 128), 1)
    columns = []
    for r in range(0, TOKENS, step):
        t = t_out[pl.ds(r, step), :]
        s = s_out[pl.ds(r, step), :]
        t_top = jnp.max(t, axis=1, keepdims=True)
        s_top = jnp.max(s, axis=1, keepdims=True)
        t_low, s_low, gap = t - t_top, s - s_top, t - s
        t_exp, s_exp = jnp.exp(t_low), jnp.exp(s_low)
        hits = lax.broadcasted_iota(jnp.int32, t.shape, 1) == label_col[r : r + step]
        values = (
            t_top,
            jnp.sum(t_exp, axis=1, keepdims=True),
            jnp.sum(t_exp * t_low, axis=1, keepdims=True),
            jnp.sum(t_exp * gap, axis=1, keepdims=True),
            s_top,
            jnp.sum(s_exp, axis=1, keepdims=True),
            jnp.sum(-s_exp * gap, axis=1, keepdims=True),
            jnp.sum(jnp.where(hits, s, 0.0), axis=1, keepdims=True),
        )
        packed = jnp.zeros((step, 128), F32)
        for k, value in enumerate(values):
            packed = jnp.where(lane == k, value, packed)
        columns.append(packed)
    table = jnp.concatenate(columns, axis=0).T[:16]
    to_natural = one_hot(tok_col[...], lanes)
    high, middle, low = split3(table)
    natural = (dot(high, to_natural) + dot(middle, to_natural)) + dot(low, to_natural)
    stats_out[...] = natural[:8]


def logits(at, blocks, tok_half, tok_col, owner, labels, tw, sw, before=None):
    tk, sk, vocab = tw.shape[0] // 2, sw.shape[0] // 2, tw.shape[1]
    tstep, sstep = tk // 4, sk // 2
    last = before is not None
    out = [
        jax.ShapeDtypeStruct((TOKENS, vocab), F32),
        jax.ShapeDtypeStruct((TOKENS, vocab), F32),
        jax.ShapeDtypeStruct((TOKENS, sk), BF16),
    ]
    if last:
        out.append(jax.ShapeDtypeStruct((8, TOKENS), F32))
    args = [at, *blocks, tok_half, tok_col, owner, labels, tw, sw, *(before or ())]
    specs = [SMEM] + [VMEM] * 8 + [ANY] * 2 + [VMEM] * (2 if last else 0)
    return pl.pallas_call(
        functools.partial(logits_kernel, (tk, sk, tstep, sstep), last),
        out_shape=out,
        in_specs=specs,
        out_specs=[VMEM] * len(out),
        scratch_shapes=[
            pltpu.VMEM((TOKENS, tk + sk), BF16),
            pltpu.VMEM((tk, vocab), BF16),
            pltpu.VMEM((sk, vocab), BF16),
            pltpu.SemaphoreType.DMA((4,)),
            pltpu.SemaphoreType.DMA((2,)),
        ],
        compiler_params=pltpu.CompilerParams(vmem_limit_bytes=44 << 20),
        cost_estimate=pl.CostEstimate(
            flops=2 * TOKENS * (tk + sk) * (vocab + TOKENS), bytes_accessed=2 * (tk + sk) * (vocab + TOKENS), transcendentals=0
        ),
        name="logits_last" if last else "logits_first",
    )(*args)


def grad_kernel(vocab, at_ref, t_ref, s_ref, stats, tok_col, tok_row, send_col, labels, sw, grads_out, send_out, loss_out, sbuf, sem):
    base = at_ref[1]
    sk = sbuf.shape[0]
    rows = pl.ds(pl.multiple_of(at_ref[2] * sk, sk), sk)
    copy = pltpu.make_async_copy(sw.at[rows, :], sbuf, sem.at[0])
    copy.start()
    t_top, t_sum, t_moment, t_gap, s_top, s_sum, s_gap, hit = (stats[k : k + 1, :] for k in range(8))
    t_log, s_log = jnp.log(t_sum), jnp.log(s_sum)
    t_lse, s_lse = t_top + t_log, s_top + s_log
    weight = (t_log - t_moment / t_sum) / math.log(vocab)
    forward = t_gap / t_sum - t_lse + s_lse
    reverse = s_gap / s_sum - s_lse + t_lse
    loss_out[...] = weight * forward + (1.0 - weight) * reverse + (s_lse - hit)
    table = jnp.concatenate([t_lse, s_lse, weight, reverse] * 2, axis=0)
    lanes = lax.broadcasted_iota(jnp.int32, (1, TOKENS), 1)
    from_natural = one_hot(tok_col[...], lanes)
    label_col = pick_column(tok_col[...], lanes, labels[...]).astype(jnp.int32) - base
    high, middle, low = split3(table)
    local = (dot_nt(from_natural, high) + dot_nt(from_natural, middle)) + dot_nt(from_natural, low)
    step = 64
    for r in range(0, TOKENS, step):
        t_lse, s_lse, weight, reverse = (local[r : r + step, k : k + 1] for k in range(4))
        t_log = t_ref[pl.ds(r, step), :] - t_lse
        s_log = s_ref[pl.ds(r, step), :] - s_lse
        t_prob, s_prob = jnp.exp(t_log), jnp.exp(s_log)
        mixed = weight * (s_prob - t_prob) + (1.0 - weight) * s_prob * (s_log - t_log - reverse)
        hits = lax.broadcasted_iota(jnp.int32, t_log.shape, 1) == label_col[r : r + step]
        mixed = mixed + s_prob - jnp.where(hits, 1.0, 0.0)
        grads_out[pl.ds(r, step), :] = (mixed / TOKENS).astype(BF16)
    ordered = dot(one_hot(send_col[...], tok_row[...]), grads_out[...]).astype(BF16)
    copy.wait()
    send_out[...] = dot_nt(ordered, sbuf[...]).astype(BF16)


def keep_kernel(at_ref, grads, tok_row, keep_col, sw, keep_out, sbuf, sem):
    sk = sbuf.shape[0]
    rows = pl.ds(pl.multiple_of(at_ref[0] * sk, sk), sk)
    copy = pltpu.make_async_copy(sw.at[rows, :], sbuf, sem.at[0])
    copy.start()
    ordered = dot(one_hot(keep_col[...], tok_row[...]), grads[...]).astype(BF16)
    copy.wait()
    keep_out[...] = dot_nt(ordered, sbuf[...])


def merge(tables):
    t_top = functools.reduce(jnp.maximum, [v[0] for v in tables])
    s_top = functools.reduce(jnp.maximum, [v[4] for v in tables])
    total = 0.0
    for v in tables:
        t_low, s_low = v[0] - t_top, v[4] - s_top
        t_scale, s_scale = jnp.exp(t_low), jnp.exp(s_low)
        total += jnp.stack(
            [
                jnp.zeros_like(t_top), t_scale * v[1], t_scale * (v[2] + t_low * v[1]), t_scale * v[3],
                jnp.zeros_like(s_top), s_scale * v[5], s_scale * v[6], v[7],
            ]
        )
    row = lax.broadcasted_iota(jnp.int32, total.shape, 0)
    return jnp.where(row == 0, t_top, jnp.where(row == 4, s_top, total))


def shards(teacher_hidden, teacher_head, student_hidden, student_head, labels, owner_map):
    me = coords(lax.axis_index(AXES))
    core = me["c"]
    local_vocab = teacher_head.shape[1]
    tk, sk = teacher_head.shape[0] // 2, student_head.shape[0] // 2
    orders = [token_order(me, half) for half in range(2)]
    own_order = jnp.where(core == 0, orders[0], orders[1])
    other_order = jnp.where(core == 0, orders[1], orders[0])
    tok_col, tok_row = orders[0][:, None], orders[0][None, :]
    base = lax.axis_index(AXES) * local_vocab
    at_own = jnp.stack([core, base, 1 - core]).astype(jnp.int32)
    at_other = jnp.stack([1 - core, base, core]).astype(jnp.int32)
    label_row, owner_row = labels[None, :], owner_map[None, :]

    halves = [
        jnp.concatenate([teacher_hidden[:, h * tk : (h + 1) * tk], student_hidden[:, h * sk : (h + 1) * sk]], axis=1) for h in range(2)
    ]
    keep = jnp.where(core == 0, halves[0], halves[1])
    send = jnp.where(core == 0, halves[1], halves[0])
    block = jnp.concatenate([keep, swap(send)], axis=0)
    for stage in range(2):
        block = jnp.concatenate([block] + [shift(block, stage, k) for k in (1, 2, 3)], axis=0)
    own_blocks = [block] + [shift(block, 2, k) for k in (1, 2, 3)]
    other_blocks = [swap(v) for v in own_blocks]

    args = (tok_col, owner_row, label_row, teacher_head, student_head)
    t_part, s_part, h_own = logits(at_own, own_blocks, own_order[None, :], *args)
    t_logits, s_logits, h_other, stats = logits(at_other, other_blocks, other_order[None, :], *args, before=(t_part, s_part))

    stats = merge([stats, swap(stats)])
    for dim in ("y", "x", "z"):
        stats = merge([stats] + [shift_dim(stats, dim, k) for k in (1, 2, 3)])

    vmem = [SMEM] + [VMEM] * 7 + [ANY]
    weights = pltpu.VMEM((sk, local_vocab), BF16)
    grads, to_other, loss = pl.pallas_call(
        functools.partial(grad_kernel, local_vocab * DEVICES),
        out_shape=[
            jax.ShapeDtypeStruct((TOKENS, local_vocab), BF16),
            jax.ShapeDtypeStruct((TOKENS, sk), BF16),
            jax.ShapeDtypeStruct((1, TOKENS), F32),
        ],
        in_specs=vmem,
        out_specs=[VMEM] * 3,
        scratch_shapes=[weights, pltpu.SemaphoreType.DMA((1,))],
        compiler_params=pltpu.CompilerParams(vmem_limit_bytes=32 << 20),
        cost_estimate=pl.CostEstimate(flops=2 * TOKENS * sk * local_vocab, bytes_accessed=4 << 20, transcendentals=0),
        name="gradient",
    )(at_own, t_logits, s_logits, stats, tok_col, tok_row, other_order[:, None], label_row, student_head)
    kept = pl.pallas_call(
        keep_kernel,
        out_shape=jax.ShapeDtypeStruct((TOKENS, sk), F32),
        in_specs=[SMEM] + [VMEM] * 3 + [ANY],
        out_specs=VMEM,
        scratch_shapes=[weights, pltpu.SemaphoreType.DMA((1,))],
        compiler_params=pltpu.CompilerParams(vmem_limit_bytes=32 << 20),
        cost_estimate=pl.CostEstimate(flops=2 * TOKENS * sk * local_vocab, bytes_accessed=4 << 20, transcendentals=0),
        name="kept",
    )(at_own, grads, tok_row, own_order[:, None], student_head)

    total = kept + swap(to_other).astype(F32)
    for stage in (2, 1, 0):
        size = total.shape[0] // 4
        parts = [shift(total[k * size : (k + 1) * size].astype(BF16), stage, -k) for k in (1, 2, 3)]
        total = total[:size] + sum(p.astype(F32) for p in parts)
    result = total.astype(BF16)
    mine, theirs = result[:ROWS], swap(result[ROWS:])
    grad_hidden = jnp.where(core == 0, jnp.concatenate([mine, theirs], axis=1), jnp.concatenate([theirs, mine], axis=1))

    ordered = jnp.where(core == 0, jnp.concatenate([h_own, h_other], axis=1), jnp.concatenate([h_other, h_own], axis=1))
    grad_head = lax.dot_general(ordered, grads, (((0,), (0,)), ((), ())), preferred_element_type=F32).astype(BF16)
    token_loss = lax.dynamic_slice_in_dim(loss[0], lax.axis_index(AXES) * ROWS, ROWS)
    return token_loss, grad_head, grad_hidden


def solution(mesh):
    in_specs = (P(AXES, None), P(None, AXES), P(AXES, None), P(None, AXES), P(), P())
    out_specs = (P(AXES), P(None, AXES), P(AXES, None))
    return jax.shard_map(shards, mesh=mesh, in_specs=in_specs, out_specs=out_specs, check_vma=False)
```

```python
import functools
import math

import jax
import jax.numpy as jnp
from jax import lax
from jax.experimental import pallas as pl
from jax.experimental.pallas import tpu as pltpu
from jax.sharding import PartitionSpec as P


AXES = ("grp", "tp")
DEVICES = 128
TOKENS = 384
ROWS = 3
HALF = TOKENS // 2
BF16 = jnp.bfloat16
F32 = jnp.float32
VMEM = pl.BlockSpec(memory_space=pltpu.VMEM)
SMEM = pl.BlockSpec(memory_space=pltpu.SMEM)
HBM = pl.BlockSpec(memory_space=pltpu.HBM)
STAGES = (("y", "x", "z"), ("z", "y", "x"))


def coords(d):
    return {"zl": d // 64, "c": d // 32 % 2, "zh": d // 16 % 2, "x": d // 4 % 4, "y": d % 4, "z": d // 16 % 2 * 2 + d // 64}


def device(c, x, y, z):
    return ((z % 2 * 2 + c) * 2 + z // 2) * 16 + x * 4 + y


def moved(d, dim, k):
    at = coords(d)
    at[dim] = (at[dim] + k) % 4
    return device(at["c"], at["x"], at["y"], at["z"])


def swap(value):
    return lax.ppermute(value, AXES, [(d, d ^ 32) for d in range(DEVICES)])


def shift(value, stage, k):
    pairs = [(d, moved(d, STAGES[coords(d)["c"]][stage], k)) for d in range(DEVICES)]
    return lax.ppermute(value, AXES, pairs)


def token_order(me):
    j = lax.iota(jnp.int32, TOKENS)
    r = j % HALF
    steps = (r // 3 % 4, r // 12 % 4, r // 48)
    tokens = []
    for core in range(2):
        at = {dim: (me[dim] - step) % 4 for dim, step in zip(STAGES[core], steps)}
        tokens.append(device(core, at["x"], at["y"], at["z"]) * ROWS + r % ROWS)
    first = (j < HALF) == (me["c"] == 0)
    return jnp.where(first, tokens[0], tokens[1])[None, :]


def split3(v):
    high = v.astype(BF16)
    rest = v - high.astype(F32)
    middle = rest.astype(BF16)
    return high, middle, (rest - middle.astype(F32)).astype(BF16)


def one_hot(column, row):
    return jnp.where(column == row, 1.0, 0.0).astype(BF16)


def dot(a, b):
    return jnp.dot(a, b, preferred_element_type=F32)


def dot_nt(a, b):
    return lax.dot_general(a, b, (((1,), (1,)), ((), ())), preferred_element_type=F32)


def lane_ids():
    return lax.broadcasted_iota(jnp.int32, (TOKENS, TOKENS), 1)


def to_column(row):
    same = lax.broadcasted_iota(jnp.int32, (TOKENS, TOKENS), 0) == lane_ids()
    return jnp.sum(jnp.where(same, row.astype(F32), 0.0), axis=1, keepdims=True).astype(jnp.int32)


def pick_column(column, row_values):
    return jnp.sum(jnp.where(column == lane_ids(), row_values.astype(F32), 0.0), axis=1, keepdims=True).astype(jnp.int32)


def teacher_kernel(n, *refs):
    blocks, (tok_row, owner, w, out, wbuf, sem) = refs[:n], refs[n:]
    slots, chunk, _ = wbuf.shape
    count = w.shape[0] // chunk

    def copy(i):
        slot = i % slots
        return pltpu.make_async_copy(w.at[pl.ds(i * chunk, chunk), :], wbuf.at[slot], sem.at[slot])

    for i in range(slots):
        copy(i).start()
    for i in range(count):
        columns = slice(i * chunk, (i + 1) * chunk)
        rows = jnp.concatenate([block[:, columns] for block in blocks], axis=0)
        copy(i).wait()
        part = dot(rows, wbuf[i % slots])
        out[...] = part if i == 0 else out[...] + part
        if i + slots < count:
            copy(i + slots).start()
    owner_col = pick_column(to_column(tok_row[...]), owner[...])
    pick = one_hot(owner_col, tok_row[...])
    high, middle, low = split3(out[...])
    out[...] = (dot(pick, high) + dot(pick, middle)) + dot(pick, low)


def student_kernel(n, *refs):
    blocks, (at_ref, t_ref, tok_row, labels, w, s_out, g_out, stats_out, g, wbuf, table, label_at, sem) = refs[:n], refs[n:]
    chunk = 896
    count = w.shape[0] // chunk

    def copy(i):
        rows = pl.ds(pl.multiple_of(i * chunk, chunk), chunk)
        return pltpu.make_async_copy(w.at[rows, :], wbuf.at[rows, :], sem.at[i])

    for i in range(count):
        copy(i).start()
    at = 0
    for block in blocks:
        g[pl.ds(at, block.shape[0]), :] = block[...]
        at += block.shape[0]
    save = pltpu.make_async_copy(g, g_out, sem.at[count])
    save.start()
    s_out[...] = jnp.zeros_like(s_out)
    tok_col = to_column(tok_row[...])
    label_at[...] = pick_column(tok_col, labels[...]) - at_ref[0]

    @pl.loop(0, count)
    def _(i):
        rows = pl.ds(pl.multiple_of(i * chunk, chunk), chunk)
        copy(i).wait()
        s_out[...] += dot(g[:, rows], wbuf[rows, :])

    step = 32
    lane = lax.broadcasted_iota(jnp.int32, (step, 128), 1)

    @pl.loop(0, TOKENS // step)
    def _(i):
        rows = pl.ds(pl.multiple_of(i * step, step), step)
        t = t_ref[rows, :]
        s = s_out[rows, :]
        t_top = jnp.max(t, axis=1, keepdims=True)
        s_top = jnp.max(s, axis=1, keepdims=True)
        t_low, s_low, gap = t - t_top, s - s_top, t - s
        t_exp, s_exp = jnp.exp(t_low), jnp.exp(s_low)
        hits = lax.broadcasted_iota(jnp.int32, t.shape, 1) == label_at[rows, :]
        values = (
            t_top,
            jnp.sum(t_exp, axis=1, keepdims=True),
            jnp.sum(t_exp * t_low, axis=1, keepdims=True),
            jnp.sum(t_exp * gap, axis=1, keepdims=True),
            s_top,
            jnp.sum(s_exp, axis=1, keepdims=True),
            jnp.sum(-s_exp * gap, axis=1, keepdims=True),
            jnp.sum(jnp.where(hits, s, 0.0), axis=1, keepdims=True),
        )
        packed = jnp.zeros((step, 128), F32)
        for k, value in enumerate(values):
            packed = jnp.where(lane == k, value, packed)
        table[rows, :] = packed

    to_natural = one_hot(tok_col, lane_ids())
    high, middle, low = split3(table[...].T[:16])
    stats_out[...] = ((dot(high, to_natural) + dot(middle, to_natural)) + dot(low, to_natural))[:8]
    save.wait()


def weight_copies(w, wbuf, sem):
    chunk = 896
    slices = [slice(i * chunk, (i + 1) * chunk) for i in range(w.shape[0] // chunk)]
    copies = [(rows, pltpu.make_async_copy(w.at[rows, :], wbuf.at[rows, :], sem.at[i])) for i, rows in enumerate(slices)]
    for _, copy in copies:
        copy.start()
    return copies


def gradient_kernel(vocab, at_ref, t_ref, s_ref, stats, tok_row, labels, w, grads_out, send_out, loss_out, local, label_at, wbuf, sem):
    copies = weight_copies(w, wbuf, sem)
    t_top, t_sum, t_moment, t_gap, s_top, s_sum, s_gap, hit = (stats[k : k + 1, :] for k in range(8))
    t_log, s_log = jnp.log(t_sum), jnp.log(s_sum)
    t_lse, s_lse = t_top + t_log, s_top + s_log
    weight = (t_log - t_moment / t_sum) / math.log(vocab)
    forward = t_gap / t_sum - t_lse + s_lse
    reverse = s_gap / s_sum - s_lse + t_lse
    loss_out[...] = weight * forward + (1.0 - weight) * reverse + (s_lse - hit)
    rows8 = jnp.concatenate([t_lse, s_lse, weight, reverse] * 2, axis=0)
    tok_col = to_column(tok_row[...])
    from_natural = one_hot(tok_col, lane_ids())
    label_at[...] = pick_column(tok_col, labels[...]) - at_ref[0]
    high, middle, low = split3(rows8)
    local[...] = (dot_nt(from_natural, high) + dot_nt(from_natural, middle)) + dot_nt(from_natural, low)
    step = 32

    @pl.loop(0, TOKENS // step)
    def _(i):
        rows = pl.ds(pl.multiple_of(i * step, step), step)
        t_lse, s_lse, weight, reverse = (local[rows, k : k + 1] for k in range(4))
        t_log = t_ref[rows, :] - t_lse
        s_log = s_ref[rows, :] - s_lse
        t_prob, s_prob = jnp.exp(t_log), jnp.exp(s_log)
        mixed = weight * (s_prob - t_prob) + (1.0 - weight) * s_prob * (s_log - t_log - reverse)
        hits = lax.broadcasted_iota(jnp.int32, t_log.shape, 1) == label_at[rows, :]
        mixed = mixed + s_prob - jnp.where(hits, 1.0, 0.0)
        grads_out[rows, :] = (mixed / TOKENS).astype(BF16)

    for rows, copy in copies:
        copy.wait()
        send_out[:, rows] = dot_nt(grads_out[HALF:, :], wbuf[rows, :]).astype(BF16)


def keep_kernel(grads, w, out, wbuf, sem):
    for rows, copy in weight_copies(w, wbuf, sem):
        copy.wait()
        out[:, rows] = dot_nt(grads[:HALF, :], wbuf[rows, :])


def call(kernel, out, specs, args, scratch, vmem, flops, out_specs=None):
    return pl.pallas_call(
        kernel,
        out_shape=[jax.ShapeDtypeStruct(*o) for o in out],
        in_specs=specs,
        out_specs=out_specs or [VMEM] * len(out),
        scratch_shapes=scratch,
        compiler_params=pltpu.CompilerParams(vmem_limit_bytes=vmem << 20),
        cost_estimate=pl.CostEstimate(flops=flops, bytes_accessed=4 << 20, transcendentals=0),
    )(*args)


def merge(tables):
    t_top = functools.reduce(jnp.maximum, [v[0] for v in tables])
    s_top = functools.reduce(jnp.maximum, [v[4] for v in tables])
    total = 0.0
    for v in tables:
        t_low, s_low = v[0] - t_top, v[4] - s_top
        t_scale, s_scale = jnp.exp(t_low), jnp.exp(s_low)
        total += jnp.stack(
            [
                jnp.zeros_like(t_top), t_scale * v[1], t_scale * (v[2] + t_low * v[1]), t_scale * v[3],
                jnp.zeros_like(s_top), s_scale * v[5], s_scale * v[6], v[7],
            ]
        )
    row = lax.broadcasted_iota(jnp.int32, total.shape, 0)
    return jnp.where(row == 0, t_top, jnp.where(row == 4, s_top, total))


def ring_shift(value, dim):
    return lax.ppermute(value, AXES, [(d, moved(d, dim, -1 if coords(d)["c"] else 1)) for d in range(DEVICES)])


def across(value, dim):
    return lax.ppermute(value, AXES, [(d, moved(d, dim, 2)) for d in range(DEVICES)])


def shards(teacher_hidden, teacher_head, student_hidden, student_head, labels, owner_map):
    me = coords(lax.axis_index(AXES))
    vocab = teacher_head.shape[1]
    tk, sk = teacher_head.shape[0], student_head.shape[0]
    tok_row = token_order(me)
    at = (lax.axis_index(AXES) * vocab).astype(jnp.int32)[None]
    label_row, owner_row = labels[None, :], owner_map[None, :]

    block = jnp.concatenate([teacher_hidden, student_hidden], axis=1)
    block = jnp.concatenate([block] + [shift(block, 0, k) for k in (1, 2, 3)], axis=0)
    parts = [block] + [shift(block, 1, k) for k in (1, 2, 3)]
    t0 = jnp.concatenate([v[:, :tk] for v in parts], axis=0)
    s0 = jnp.concatenate([v[:, tk:] for v in parts], axis=0)
    t1, t3 = shift(t0, 2, 1), shift(t0, 2, -1)
    t1, t3, s0 = lax.optimization_barrier((t1, t3, s0))
    rows = t0.shape[0] // 2
    t2 = [shift(t1[:rows], 2, 1), shift(t3[rows:], 2, -1)]
    s_moved = [shift(s0, 2, k) for k in (1, 2, 3)]
    t2_other = [swap(v) for v in t2]
    t_blocks = [t0, t1, *t2, t3, swap(t0), swap(t1), *t2_other, swap(t3)]

    n = len(t_blocks)
    (t_logits,) = call(
        functools.partial(teacher_kernel, n),
        [((TOKENS, vocab), F32)],
        [VMEM] * (n + 2) + [HBM],
        [*t_blocks, tok_row, owner_row, teacher_head],
        [pltpu.VMEM((3, 1024, vocab), BF16), pltpu.SemaphoreType.DMA((3,))],
        48,
        2 * TOKENS * tk * vocab,
    )
    *s_moved, t_logits = lax.optimization_barrier((*s_moved, t_logits))
    s_own = [s0, *s_moved]
    s_blocks = s_own + [swap(v) for v in s_own]
    n = len(s_blocks)
    s_logits, hidden, stats = call(
        functools.partial(student_kernel, n),
        [((TOKENS, vocab), F32), ((TOKENS, sk), BF16), ((8, TOKENS), F32)],
        [VMEM] * n + [SMEM] + [VMEM] * 3 + [HBM],
        [*s_blocks, at, t_logits, tok_row, label_row, student_head],
        [
            pltpu.VMEM((TOKENS, sk), BF16),
            pltpu.VMEM((sk, vocab), BF16),
            pltpu.VMEM((TOKENS, 128), F32),
            pltpu.VMEM((TOKENS, 1), jnp.int32),
            pltpu.SemaphoreType.DMA((5,)),
        ],
        50,
        2 * TOKENS * sk * vocab,
        [VMEM, HBM, VMEM],
    )

    stats = merge([stats, swap(stats)])
    for dim in ("y", "x", "z"):
        near, far = ring_shift(stats, dim), across(stats, dim)
        stats = merge([stats, near, swap(near), far])

    wscratch = pltpu.VMEM((sk, vocab), BF16)
    grads, to_other, loss = call(
        functools.partial(gradient_kernel, vocab * DEVICES),
        [((TOKENS, vocab), BF16), ((HALF, sk), BF16), ((1, TOKENS), F32)],
        [SMEM] + [VMEM] * 5 + [HBM],
        [at, t_logits, s_logits, stats, tok_row, label_row, student_head],
        [pltpu.VMEM((TOKENS, 8), F32), pltpu.VMEM((TOKENS, 1), jnp.int32), wscratch, pltpu.SemaphoreType.DMA((4,))],
        56,
        TOKENS * sk * vocab,
    )
    (kept,) = call(keep_kernel, [((HALF, sk), F32)], [VMEM, HBM], [grads, student_head], [wscratch, pltpu.SemaphoreType.DMA((4,))], 56, TOKENS * sk * vocab)

    total = kept + swap(to_other).astype(F32)
    for stage in (2, 1, 0):
        size = total.shape[0] // 4
        parts = [shift(total[k * size : (k + 1) * size].astype(BF16), stage, -k) for k in (1, 2, 3)]
        if stage == 2:
            grad_head = lax.dot_general(hidden, grads, (((0,), (0,)), ((), ())), preferred_element_type=F32).astype(BF16)
            total, grad_head, *parts = lax.optimization_barrier((total, grad_head, *parts))
        total = total[:size] + sum(p.astype(F32) for p in parts)
    token_loss = lax.dynamic_slice_in_dim(loss[0], lax.axis_index(AXES) * ROWS, ROWS)
    return token_loss, grad_head, total.astype(BF16)


def solution(mesh):
    in_specs = (P(AXES, None), P(None, AXES), P(AXES, None), P(None, AXES), P(), P())
    out_specs = (P(AXES), P(None, AXES), P(AXES, None))
    return jax.shard_map(shards, mesh=mesh, in_specs=in_specs, out_specs=out_specs, check_vma=False)
```

```python
import functools
import math

import jax
import jax.numpy as jnp
from jax import lax
from jax.experimental import pallas as pl
from jax.experimental.pallas import tpu as pltpu
from jax.sharding import PartitionSpec as P


AXES = ("grp", "tp")
DEVICES = 128
TOKENS = 384
ROWS = 3
HALF = TOKENS // 2
BF16 = jnp.bfloat16
F32 = jnp.float32
VMEM = pl.BlockSpec(memory_space=pltpu.VMEM)
SMEM = pl.BlockSpec(memory_space=pltpu.SMEM)
HBM = pl.BlockSpec(memory_space=pltpu.HBM)
STAGES = (("y", "x", "z"), ("z", "y", "x"))


def coords(d):
    return {"zl": d // 64, "c": d // 32 % 2, "zh": d // 16 % 2, "x": d // 4 % 4, "y": d % 4, "z": d // 16 % 2 * 2 + d // 64}


def device(c, x, y, z):
    return ((z % 2 * 2 + c) * 2 + z // 2) * 16 + x * 4 + y


def moved(d, dim, k):
    at = coords(d)
    at[dim] = (at[dim] + k) % 4
    return device(at["c"], at["x"], at["y"], at["z"])


def swap(value):
    return lax.ppermute(value, AXES, [(d, d ^ 32) for d in range(DEVICES)])


def shift(value, stage, k):
    pairs = [(d, moved(d, STAGES[coords(d)["c"]][stage], k)) for d in range(DEVICES)]
    return lax.ppermute(value, AXES, pairs)


def token_order(me):
    j = lax.iota(jnp.int32, TOKENS)
    r = j % HALF
    steps = (r // 3 % 4, r // 12 % 4, r // 48)
    tokens = []
    for core in range(2):
        at = {dim: (me[dim] - step) % 4 for dim, step in zip(STAGES[core], steps)}
        tokens.append(device(core, at["x"], at["y"], at["z"]) * ROWS + r % ROWS)
    first = (j < HALF) == (me["c"] == 0)
    return jnp.where(first, tokens[0], tokens[1])[None, :]


def split3(v):
    high = v.astype(BF16)
    rest = v - high.astype(F32)
    middle = rest.astype(BF16)
    return high, middle, (rest - middle.astype(F32)).astype(BF16)


def one_hot(column, row):
    return jnp.where(column == row, 1.0, 0.0).astype(BF16)


def dot(a, b):
    return jnp.dot(a, b, preferred_element_type=F32)


def dot_nt(a, b):
    return lax.dot_general(a, b, (((1,), (1,)), ((), ())), preferred_element_type=F32)


def lane_ids():
    return lax.broadcasted_iota(jnp.int32, (TOKENS, TOKENS), 1)


def to_column(row):
    same = lax.broadcasted_iota(jnp.int32, (TOKENS, TOKENS), 0) == lane_ids()
    return jnp.sum(jnp.where(same, row.astype(F32), 0.0), axis=1, keepdims=True).astype(jnp.int32)


def pick_column(column, row_values):
    return jnp.sum(jnp.where(column == lane_ids(), row_values.astype(F32), 0.0), axis=1, keepdims=True).astype(jnp.int32)


def teacher_kernel(n, last, *refs):
    blocks, refs = refs[:n], refs[n:]
    if last:
        (before, source, tok_row, owner, w, out, wbuf, part, sem) = refs
    else:
        (w, part, wbuf, sem) = refs
    slots, chunk, _ = wbuf.shape
    count = w.shape[0] // chunk

    def copy(i):
        slot = i % slots
        return pltpu.make_async_copy(w.at[pl.ds(i * chunk, chunk), :], wbuf.at[slot], sem.at[slot])

    for i in range(slots):
        copy(i).start()
    for i in range(count):
        columns = slice(i * chunk, (i + 1) * chunk)
        rows = jnp.concatenate([block[:, columns] for block in blocks], axis=0)
        copy(i).wait()
        value = dot(rows, wbuf[i % slots])
        part[...] = value if i == 0 else part[...] + value
        if i + slots < count:
            copy(i + slots).start()
    if not last:
        return
    owner_col = pick_column(to_column(tok_row[...]), owner[...])
    pick = one_hot(owner_col, source[...])
    high, middle, low = split3(jnp.concatenate([before[...], part[...]], axis=0))
    out[...] = (dot(pick, high) + dot(pick, middle)) + dot(pick, low)


def student_kernel(n, *refs):
    blocks, (at_ref, t_ref, tok_row, labels, w, s_out, stats_out, g, wbuf, table, label_at, sem) = refs[:n], refs[n:]
    chunk = 896
    count = w.shape[0] // chunk

    def copy(i):
        rows = pl.ds(pl.multiple_of(i * chunk, chunk), chunk)
        return pltpu.make_async_copy(w.at[rows, :], wbuf.at[rows, :], sem.at[i])

    for i in range(count):
        copy(i).start()
    at = 0
    for block in blocks:
        g[pl.ds(at, block.shape[0]), :] = block[...]
        at += block.shape[0]
    s_out[...] = jnp.zeros_like(s_out)
    tok_col = to_column(tok_row[...])
    label_at[...] = pick_column(tok_col, labels[...]) - at_ref[0]

    @pl.loop(0, count)
    def _(i):
        rows = pl.ds(pl.multiple_of(i * chunk, chunk), chunk)
        copy(i).wait()
        s_out[...] += dot(g[:, rows], wbuf[rows, :])

    step = 64
    lane = lax.broadcasted_iota(jnp.int32, (step, 128), 1)
    for i in range(TOKENS // step):
        rows = slice(i * step, (i + 1) * step)
        t = t_ref[rows, :]
        s = s_out[rows, :]
        t_top = jnp.max(t, axis=1, keepdims=True)
        s_top = jnp.max(s, axis=1, keepdims=True)
        t_low, s_low, gap = t - t_top, s - s_top, t - s
        t_exp, s_exp = jnp.exp(t_low), jnp.exp(s_low)
        hits = lax.broadcasted_iota(jnp.int32, t.shape, 1) == label_at[rows, :]
        values = (
            t_top,
            jnp.sum(t_exp, axis=1, keepdims=True),
            jnp.sum(t_exp * t_low, axis=1, keepdims=True),
            jnp.sum(t_exp * gap, axis=1, keepdims=True),
            s_top,
            jnp.sum(s_exp, axis=1, keepdims=True),
            jnp.sum(-s_exp * gap, axis=1, keepdims=True),
            jnp.sum(jnp.where(hits, s, 0.0), axis=1, keepdims=True),
        )
        packed = jnp.zeros((step, 128), F32)
        for k, value in enumerate(values):
            packed = jnp.where(lane == k, value, packed)
        table[rows, :] = packed

    to_natural = one_hot(tok_col, lane_ids())
    high, middle, low = split3(table[...].T[:16])
    stats_out[...] = ((dot(high, to_natural) + dot(middle, to_natural)) + dot(low, to_natural))[:8]


def weight_copies(w, wbuf, sem):
    chunk = 896
    slices = [slice(i * chunk, (i + 1) * chunk) for i in range(w.shape[0] // chunk)]
    copies = [(rows, pltpu.make_async_copy(w.at[rows, :], wbuf.at[rows, :], sem.at[i])) for i, rows in enumerate(slices)]
    for _, copy in copies:
        copy.start()
    return copies


def gradient_kernel(vocab, at_ref, t_ref, s_ref, stats, tok_row, labels, w, grads_out, send_out, loss_out, wbuf, local, label_at, sem):
    copies = weight_copies(w, wbuf, sem)
    t_top, t_sum, t_moment, t_gap, s_top, s_sum, s_gap, hit = (stats[k : k + 1, :] for k in range(8))
    t_log, s_log = jnp.log(t_sum), jnp.log(s_sum)
    t_lse, s_lse = t_top + t_log, s_top + s_log
    weight = (t_log - t_moment / t_sum) / math.log(vocab)
    forward = t_gap / t_sum - t_lse + s_lse
    reverse = s_gap / s_sum - s_lse + t_lse
    loss_out[...] = weight * forward + (1.0 - weight) * reverse + (s_lse - hit)
    rows8 = jnp.concatenate([t_lse, s_lse, weight, reverse] * 2, axis=0)
    tok_col = to_column(tok_row[...])
    from_natural = one_hot(tok_col, lane_ids())
    label_at[...] = pick_column(tok_col, labels[...]) - at_ref[0]
    high, middle, low = split3(rows8)
    local[...] = (dot_nt(from_natural, high) + dot_nt(from_natural, middle)) + dot_nt(from_natural, low)
    step = 64
    for i in range(TOKENS // step):
        rows = slice(i * step, (i + 1) * step)
        t_lse, s_lse, weight, reverse = (local[rows, k : k + 1] for k in range(4))
        t_log = t_ref[rows, :] - t_lse
        s_log = s_ref[rows, :] - s_lse
        t_prob, s_prob = jnp.exp(t_log), jnp.exp(s_log)
        mixed = weight * (s_prob - t_prob) + (1.0 - weight) * s_prob * (s_log - t_log - reverse)
        hits = lax.broadcasted_iota(jnp.int32, t_log.shape, 1) == label_at[rows, :]
        mixed = mixed + s_prob - jnp.where(hits, 1.0, 0.0)
        grads_out[rows, :] = (mixed / TOKENS).astype(BF16)

    for rows, copy in copies:
        copy.wait()
        send_out[:, rows] = dot_nt(grads_out[HALF:, :], wbuf[rows, :]).astype(BF16)


def keep_kernel(grads, w, out):
    chunk = 896
    for i in range(w.shape[0] // chunk):
        rows = slice(i * chunk, (i + 1) * chunk)
        out[:, rows] = dot_nt(grads[:HALF, :], w[rows, :])


def call(kernel, out, specs, args, scratch, vmem, flops, out_specs=None):
    return pl.pallas_call(
        kernel,
        out_shape=[jax.ShapeDtypeStruct(*o) for o in out],
        in_specs=specs,
        out_specs=out_specs or [VMEM] * len(out),
        scratch_shapes=scratch,
        compiler_params=pltpu.CompilerParams(vmem_limit_bytes=vmem << 20),
        cost_estimate=pl.CostEstimate(flops=flops, bytes_accessed=4 << 20, transcendentals=0),
    )(*args)


def merge(tables):
    t_top = functools.reduce(jnp.maximum, [v[0] for v in tables])
    s_top = functools.reduce(jnp.maximum, [v[4] for v in tables])
    total = 0.0
    for v in tables:
        t_low, s_low = v[0] - t_top, v[4] - s_top
        t_scale, s_scale = jnp.exp(t_low), jnp.exp(s_low)
        total += jnp.stack(
            [
                jnp.zeros_like(t_top), t_scale * v[1], t_scale * (v[2] + t_low * v[1]), t_scale * v[3],
                jnp.zeros_like(s_top), s_scale * v[5], s_scale * v[6], v[7],
            ]
        )
    row = lax.broadcasted_iota(jnp.int32, total.shape, 0)
    return jnp.where(row == 0, t_top, jnp.where(row == 4, s_top, total))


def ring_shift(value, dim):
    return lax.ppermute(value, AXES, [(d, moved(d, dim, -1 if coords(d)["c"] else 1)) for d in range(DEVICES)])


def across(value, dim):
    return lax.ppermute(value, AXES, [(d, moved(d, dim, 2)) for d in range(DEVICES)])


def shards(teacher_hidden, teacher_head, student_hidden, student_head, labels, owner_map):
    me = coords(lax.axis_index(AXES))
    vocab = teacher_head.shape[1]
    tk, sk = teacher_head.shape[0], student_head.shape[0]
    tok_row = token_order(me)
    at = (lax.axis_index(AXES) * vocab).astype(jnp.int32)[None]
    label_row, owner_row = labels[None, :], owner_map[None, :]

    parts = [teacher_hidden] + [shift(teacher_hidden, 0, k) for k in (1, 2, 3)]
    t = jnp.concatenate(parts, axis=0)
    t = jnp.concatenate([t] + [shift(t, 1, k) for k in (1, 2, 3)], axis=0)
    parts = [student_hidden] + [shift(student_hidden, 0, k) for k in (1, 2, 3)]
    s = jnp.concatenate(parts, axis=0)
    s = lax.optimization_barrier(jnp.concatenate([s] + [shift(s, 1, k) for k in (1, 2, 3)], axis=0))
    size = t.shape[0] // 2
    a, b = t[:size], t[size:]
    before_a, after_b = shift(a, 2, 1), shift(b, 2, -1)
    before_b, after_a = shift(b, 2, 1), shift(a, 2, -1)
    far = [shift(before_a, 2, 1), shift(after_b, 2, -1)]
    s_moved = [shift(s, 2, k) for k in (1, 2, 3)]
    near = [before_a, before_b, after_a, after_b]
    near_other = [swap(v) for v in near]
    near = [a, b, *near, swap(a), swap(b), *near_other]
    far = far + [swap(v) for v in far]
    s0 = s

    def teacher(last, blocks, more, specs, scratch):
        rows = sum(v.shape[0] for v in blocks)
        return call(
            functools.partial(teacher_kernel, len(blocks), last),
            [((TOKENS if last else rows, vocab), F32)],
            [VMEM] * len(blocks) + specs + [HBM],
            [*blocks, *more, teacher_head],
            [pltpu.VMEM((3, 1024, vocab), BF16), *scratch, pltpu.SemaphoreType.DMA((3,))],
            44,
            2 * rows * tk * vocab,
        )[0]

    t_first = teacher(False, near, [], [], [])
    q = HALF // 4
    pieces = [tok_row[:, at * q : (at + 1) * q] for at in (0, 1, 3, 4, 5, 7, 2, 6)]
    source = jnp.concatenate(pieces, axis=1)
    last_rows = pltpu.VMEM((sum(v.shape[0] for v in far), vocab), F32)
    t_logits = teacher(True, far, [t_first, source, tok_row, owner_row], [VMEM] * 4, [last_rows])
    *s_moved, t_logits = lax.optimization_barrier((*s_moved, t_logits))
    s_own = [s0, *s_moved]
    s_blocks = s_own + [swap(v) for v in s_own]
    n = len(s_blocks)
    s_logits, stats = call(
        functools.partial(student_kernel, n),
        [((TOKENS, vocab), F32), ((8, TOKENS), F32)],
        [VMEM] * n + [SMEM] + [VMEM] * 3 + [HBM],
        [*s_blocks, at, t_logits, tok_row, label_row, student_head],
        [
            pltpu.VMEM((TOKENS, sk), BF16),
            pltpu.VMEM((sk, vocab), BF16),
            pltpu.VMEM((TOKENS, 128), F32),
            pltpu.VMEM((TOKENS, 1), jnp.int32),
            pltpu.SemaphoreType.DMA((4,)),
        ],
        44,
        2 * TOKENS * sk * vocab,
    )

    stats = merge([stats, swap(stats)])
    for dim in ("y", "x", "z"):
        near, far = ring_shift(stats, dim), across(stats, dim)
        stats = merge([stats, near, swap(near), far])

    grads, to_other, loss, weights = call(
        functools.partial(gradient_kernel, vocab * DEVICES),
        [((TOKENS, vocab), BF16), ((HALF, sk), BF16), ((1, TOKENS), F32), ((sk, vocab), BF16)],
        [SMEM] + [VMEM] * 5 + [HBM],
        [at, t_logits, s_logits, stats, tok_row, label_row, student_head],
        [pltpu.VMEM((TOKENS, 8), F32), pltpu.VMEM((TOKENS, 1), jnp.int32), pltpu.SemaphoreType.DMA((4,))],
        52,
        TOKENS * sk * vocab,
    )
    (kept,) = call(keep_kernel, [((HALF, sk), F32)], [VMEM] * 2, [grads, weights], [], 52, TOKENS * sk * vocab)

    total = kept + swap(to_other).astype(F32)
    for stage in (2, 1, 0):
        size = total.shape[0] // 4
        parts = [shift(total[k * size : (k + 1) * size].astype(BF16), stage, -k) for k in (1, 2, 3)]
        if stage == 2:
            hidden = jnp.concatenate(s_blocks, axis=0)
            grad_head = lax.dot_general(hidden, grads, (((0,), (0,)), ((), ())), preferred_element_type=F32).astype(BF16)
            total, grad_head, *parts = lax.optimization_barrier((total, grad_head, *parts))
        total = total[:size] + sum(p.astype(F32) for p in parts)
    token_loss = lax.dynamic_slice_in_dim(loss[0], lax.axis_index(AXES) * ROWS, ROWS)
    return token_loss, grad_head, total.astype(BF16)


def solution(mesh):
    in_specs = (P(AXES, None), P(None, AXES), P(AXES, None), P(None, AXES), P(), P())
    out_specs = (P(AXES), P(None, AXES), P(AXES, None))
    return jax.shard_map(shards, mesh=mesh, in_specs=in_specs, out_specs=out_specs, check_vma=False)
```

```python
import functools
import math

import jax
import jax.numpy as jnp
from jax import lax
from jax.experimental import pallas as pl
from jax.experimental.pallas import tpu as pltpu
from jax.sharding import PartitionSpec as P


AXES = ("grp", "tp")
DEVICES = 128
TOKENS = 384
ROWS = 3
HALF = TOKENS // 2
BF16 = jnp.bfloat16
F32 = jnp.float32
VMEM = pl.BlockSpec(memory_space=pltpu.VMEM)
SMEM = pl.BlockSpec(memory_space=pltpu.SMEM)
HBM = pl.BlockSpec(memory_space=pltpu.HBM)
STAGES = (("y", "x", "z"), ("z", "y", "x"))


def coords(d):
    return {"zl": d // 64, "c": d // 32 % 2, "zh": d // 16 % 2, "x": d // 4 % 4, "y": d % 4, "z": d // 16 % 2 * 2 + d // 64}


def device(c, x, y, z):
    return ((z % 2 * 2 + c) * 2 + z // 2) * 16 + x * 4 + y


def moved(d, dim, k):
    at = coords(d)
    at[dim] = (at[dim] + k) % 4
    return device(at["c"], at["x"], at["y"], at["z"])


def swap(value):
    return lax.ppermute(value, AXES, [(d, d ^ 32) for d in range(DEVICES)])


def shift(value, stage, k):
    pairs = [(d, moved(d, STAGES[coords(d)["c"]][stage], k)) for d in range(DEVICES)]
    return lax.ppermute(value, AXES, pairs)


def token_order(me):
    j = lax.iota(jnp.int32, TOKENS)
    r = j % HALF
    steps = (r // 3 % 4, r // 12 % 4, r // 48)
    tokens = []
    for core in range(2):
        at = {dim: (me[dim] - step) % 4 for dim, step in zip(STAGES[core], steps)}
        tokens.append(device(core, at["x"], at["y"], at["z"]) * ROWS + r % ROWS)
    first = (j < HALF) == (me["c"] == 0)
    return jnp.where(first, tokens[0], tokens[1])[None, :]


def split3(v):
    high = v.astype(BF16)
    rest = v - high.astype(F32)
    middle = rest.astype(BF16)
    return high, middle, (rest - middle.astype(F32)).astype(BF16)


def one_hot(column, row):
    return jnp.where(column == row, 1.0, 0.0).astype(BF16)


def dot(a, b):
    return jnp.dot(a, b, preferred_element_type=F32)


def dot_nt(a, b):
    return lax.dot_general(a, b, (((1,), (1,)), ((), ())), preferred_element_type=F32)


def lane_ids():
    return lax.broadcasted_iota(jnp.int32, (TOKENS, TOKENS), 1)


def to_column(row):
    same = lax.broadcasted_iota(jnp.int32, (TOKENS, TOKENS), 0) == lane_ids()
    return jnp.sum(jnp.where(same, row.astype(F32), 0.0), axis=1, keepdims=True).astype(jnp.int32)


def pick_column(column, row_values):
    return jnp.sum(jnp.where(column == lane_ids(), row_values.astype(F32), 0.0), axis=1, keepdims=True).astype(jnp.int32)


def teacher_kernel(n, *refs):
    blocks, (source, tok_row, owner, w, out, wbuf, sem) = refs[:n], refs[n:]
    slots, chunk, _ = wbuf.shape
    count = w.shape[0] // chunk

    def copy(i):
        slot = i % slots
        return pltpu.make_async_copy(w.at[pl.ds(i * chunk, chunk), :], wbuf.at[slot], sem.at[slot])

    for i in range(slots):
        copy(i).start()
    for i in range(count):
        columns = slice(i * chunk, (i + 1) * chunk)
        rows = jnp.concatenate([block[:, columns] for block in blocks], axis=0)
        copy(i).wait()
        part = dot(rows, wbuf[i % slots])
        out[...] = part if i == 0 else out[...] + part
        if i + slots < count:
            copy(i + slots).start()
    owner_col = pick_column(to_column(tok_row[...]), owner[...])
    pick = one_hot(owner_col, source[...])
    high, middle, low = split3(out[...])
    out[...] = (dot(pick, high) + dot(pick, middle)) + dot(pick, low)


def student_kernel(n, *refs):
    blocks, refs = refs[:n], refs[n:]
    at_ref, t_ref, tok_row, labels, w, s_save, t_save, g_save, stats_out, s_out, g, wbuf, table, label_at, sem = refs
    chunk = 896
    count = w.shape[0] // chunk

    def copy(i):
        rows = pl.ds(pl.multiple_of(i * chunk, chunk), chunk)
        return pltpu.make_async_copy(w.at[rows, :], wbuf.at[rows, :], sem.at[i])

    for i in range(count):
        copy(i).start()
    at = 0
    for block in blocks:
        g[pl.ds(at, block.shape[0]), :] = block[...]
        at += block.shape[0]
    saves = [pltpu.make_async_copy(*pair, sem.at[count + i]) for i, pair in enumerate([(t_ref, t_save), (g, g_save), (s_out, s_save)])]
    saves[0].start()
    saves[1].start()
    s_out[...] = jnp.zeros_like(s_out)
    tok_col = to_column(tok_row[...])
    label_at[...] = pick_column(tok_col, labels[...]) - at_ref[0]

    @pl.loop(0, count)
    def _(i):
        rows = pl.ds(pl.multiple_of(i * chunk, chunk), chunk)
        copy(i).wait()
        s_out[...] += dot(g[:, rows], wbuf[rows, :])

    saves[2].start()
    step = 64
    lane = lax.broadcasted_iota(jnp.int32, (step, 128), 1)
    for i in range(TOKENS // step):
        rows = slice(i * step, (i + 1) * step)
        t = t_ref[rows, :]
        s = s_out[rows, :]
        t_top = jnp.max(t, axis=1, keepdims=True)
        s_top = jnp.max(s, axis=1, keepdims=True)
        t_low, s_low, gap = t - t_top, s - s_top, t - s
        t_exp, s_exp = jnp.exp(t_low), jnp.exp(s_low)
        hits = lax.broadcasted_iota(jnp.int32, t.shape, 1) == label_at[rows, :]
        values = (
            t_top,
            jnp.sum(t_exp, axis=1, keepdims=True),
            jnp.sum(t_exp * t_low, axis=1, keepdims=True),
            jnp.sum(t_exp * gap, axis=1, keepdims=True),
            s_top,
            jnp.sum(s_exp, axis=1, keepdims=True),
            jnp.sum(-s_exp * gap, axis=1, keepdims=True),
            jnp.sum(jnp.where(hits, s, 0.0), axis=1, keepdims=True),
        )
        packed = jnp.zeros((step, 128), F32)
        for k, value in enumerate(values):
            packed = jnp.where(lane == k, value, packed)
        table[rows, :] = packed

    to_natural = one_hot(tok_col, lane_ids())
    high, middle, low = split3(table[...].T[:16])
    stats_out[...] = ((dot(high, to_natural) + dot(middle, to_natural)) + dot(low, to_natural))[:8]
    for save in saves:
        save.wait()


def weight_copies(w, wbuf, sem):
    chunk = 896
    slices = [slice(i * chunk, (i + 1) * chunk) for i in range(w.shape[0] // chunk)]
    copies = [(rows, pltpu.make_async_copy(w.at[rows, :], wbuf.at[rows, :], sem.at[i])) for i, rows in enumerate(slices)]
    for _, copy in copies:
        copy.start()
    return copies


def gradient_kernel(vocab, at_ref, t_in, s_in, stats, tok_row, labels, w, grads_out, send_out, keep_out, loss_out, t_ref, s_ref, wbuf, local, label_at, sem):
    loads = [pltpu.make_async_copy(*pair, sem.at[4 + i]) for i, pair in enumerate([(t_in, t_ref), (s_in, s_ref)])]
    for load in loads:
        load.start()
    copies = weight_copies(w, wbuf, sem)
    t_top, t_sum, t_moment, t_gap, s_top, s_sum, s_gap, hit = (stats[k : k + 1, :] for k in range(8))
    t_log, s_log = jnp.log(t_sum), jnp.log(s_sum)
    t_lse, s_lse = t_top + t_log, s_top + s_log
    weight = (t_log - t_moment / t_sum) / math.log(vocab)
    forward = t_gap / t_sum - t_lse + s_lse
    reverse = s_gap / s_sum - s_lse + t_lse
    loss_out[...] = weight * forward + (1.0 - weight) * reverse + (s_lse - hit)
    rows8 = jnp.concatenate([t_lse, s_lse, weight, reverse] * 2, axis=0)
    tok_col = to_column(tok_row[...])
    from_natural = one_hot(tok_col, lane_ids())
    label_at[...] = pick_column(tok_col, labels[...]) - at_ref[0]
    high, middle, low = split3(rows8)
    local[...] = (dot_nt(from_natural, high) + dot_nt(from_natural, middle)) + dot_nt(from_natural, low)
    for load in loads:
        load.wait()
    step = 64
    for i in range(TOKENS // step):
        rows = slice(i * step, (i + 1) * step)
        t_lse, s_lse, weight, reverse = (local[rows, k : k + 1] for k in range(4))
        t_log = t_ref[rows, :] - t_lse
        s_log = s_ref[rows, :] - s_lse
        t_prob, s_prob = jnp.exp(t_log), jnp.exp(s_log)
        mixed = weight * (s_prob - t_prob) + (1.0 - weight) * s_prob * (s_log - t_log - reverse)
        hits = lax.broadcasted_iota(jnp.int32, t_log.shape, 1) == label_at[rows, :]
        mixed = mixed + s_prob - jnp.where(hits, 1.0, 0.0)
        grads_out[rows, :] = (mixed / TOKENS).astype(BF16)

    for rows, copy in copies:
        copy.wait()
        part = dot_nt(grads_out[...], wbuf[rows, :])
        send_out[:, rows] = part[HALF:].astype(BF16)
        keep_out[:, rows] = part[:HALF]


def call(kernel, out, specs, args, scratch, vmem, flops, out_specs=None):
    return pl.pallas_call(
        kernel,
        out_shape=[jax.ShapeDtypeStruct(*o) for o in out],
        in_specs=specs,
        out_specs=out_specs or [VMEM] * len(out),
        scratch_shapes=scratch,
        compiler_params=pltpu.CompilerParams(vmem_limit_bytes=vmem << 20),
        cost_estimate=pl.CostEstimate(flops=flops, bytes_accessed=4 << 20, transcendentals=0),
    )(*args)


def merge(tables):
    t_top = functools.reduce(jnp.maximum, [v[0] for v in tables])
    s_top = functools.reduce(jnp.maximum, [v[4] for v in tables])
    total = 0.0
    for v in tables:
        t_low, s_low = v[0] - t_top, v[4] - s_top
        t_scale, s_scale = jnp.exp(t_low), jnp.exp(s_low)
        total += jnp.stack(
            [
                jnp.zeros_like(t_top), t_scale * v[1], t_scale * (v[2] + t_low * v[1]), t_scale * v[3],
                jnp.zeros_like(s_top), s_scale * v[5], s_scale * v[6], v[7],
            ]
        )
    row = lax.broadcasted_iota(jnp.int32, total.shape, 0)
    return jnp.where(row == 0, t_top, jnp.where(row == 4, s_top, total))


def ring_shift(value, dim):
    return lax.ppermute(value, AXES, [(d, moved(d, dim, -1 if coords(d)["c"] else 1)) for d in range(DEVICES)])


def across(value, dim):
    return lax.ppermute(value, AXES, [(d, moved(d, dim, 2)) for d in range(DEVICES)])


def shards(teacher_hidden, teacher_head, student_hidden, student_head, labels, owner_map):
    me = coords(lax.axis_index(AXES))
    vocab = teacher_head.shape[1]
    tk, sk = teacher_head.shape[0], student_head.shape[0]
    tok_row = token_order(me)
    at = (lax.axis_index(AXES) * vocab).astype(jnp.int32)[None]
    label_row, owner_row = labels[None, :], owner_map[None, :]

    parts = [teacher_hidden] + [shift(teacher_hidden, 0, k) for k in (1, 2, 3)]
    t = jnp.concatenate(parts, axis=0)
    t = jnp.concatenate([t] + [shift(t, 1, k) for k in (1, 2, 3)], axis=0)
    parts = [student_hidden] + [shift(student_hidden, 0, k) for k in (1, 2, 3)]
    s = jnp.concatenate(parts, axis=0)
    s = lax.optimization_barrier(jnp.concatenate([s] + [shift(s, 1, k) for k in (1, 2, 3)], axis=0))
    size = t.shape[0] // 2
    a, b = t[:size], t[size:]
    before_a, after_b = shift(a, 2, 1), shift(b, 2, -1)
    before_b, after_a = shift(b, 2, 1), shift(a, 2, -1)
    far = [shift(before_a, 2, 1), shift(after_b, 2, -1)]
    s_moved = [shift(s, 2, k) for k in (1, 2, 3)]
    near = [before_a, before_b, after_a, after_b]
    near = [a, b, *near, swap(a), swap(b), *[swap(v) for v in near]]
    far = far + [swap(v) for v in far]
    s0 = s

    blocks = near + far
    q = HALF // 4
    pieces = [tok_row[:, at * q : (at + 1) * q] for at in (0, 1, 3, 4, 5, 7, 2, 6)]
    source = jnp.concatenate(pieces, axis=1)
    (t_logits,) = call(
        functools.partial(teacher_kernel, len(blocks)),
        [((TOKENS, vocab), F32)],
        [VMEM] * (len(blocks) + 3) + [HBM],
        [*blocks, source, tok_row, owner_row, teacher_head],
        [pltpu.VMEM((3, 1024, vocab), BF16), pltpu.SemaphoreType.DMA((3,))],
        44,
        2 * TOKENS * tk * vocab,
    )
    *s_moved, t_logits = lax.optimization_barrier((*s_moved, t_logits))
    s_own = [s0, *s_moved]
    s_blocks = s_own + [swap(v) for v in s_own]
    n = len(s_blocks)
    s_logits, t_logits, hidden, stats = call(
        functools.partial(student_kernel, n),
        [((TOKENS, vocab), F32), ((TOKENS, vocab), F32), ((TOKENS, sk), BF16), ((8, TOKENS), F32)],
        [VMEM] * n + [SMEM] + [VMEM] * 3 + [HBM],
        [*s_blocks, at, t_logits, tok_row, label_row, student_head],
        [
            pltpu.VMEM((TOKENS, vocab), F32),
            pltpu.VMEM((TOKENS, sk), BF16),
            pltpu.VMEM((sk, vocab), BF16),
            pltpu.VMEM((TOKENS, 128), F32),
            pltpu.VMEM((TOKENS, 1), jnp.int32),
            pltpu.SemaphoreType.DMA((7,)),
        ],
        50,
        2 * TOKENS * sk * vocab,
        [HBM, HBM, HBM, VMEM],
    )

    stats = merge([stats, swap(stats)])
    for dim in ("y", "x", "z"):
        near, far = ring_shift(stats, dim), across(stats, dim)
        stats = merge([stats, near, swap(near), far])

    grads, to_other, kept, loss = call(
        functools.partial(gradient_kernel, vocab * DEVICES),
        [((TOKENS, vocab), BF16), ((HALF, sk), BF16), ((HALF, sk), F32), ((1, TOKENS), F32)],
        [SMEM] + [HBM] * 2 + [VMEM] * 3 + [HBM],
        [at, t_logits, s_logits, stats, tok_row, label_row, student_head],
        [
            pltpu.VMEM((TOKENS, vocab), F32),
            pltpu.VMEM((TOKENS, vocab), F32),
            pltpu.VMEM((sk, vocab), BF16),
            pltpu.VMEM((TOKENS, 8), F32),
            pltpu.VMEM((TOKENS, 1), jnp.int32),
            pltpu.SemaphoreType.DMA((6,)),
        ],
        44,
        2 * TOKENS * sk * vocab,
    )

    received = swap(to_other)
    grad_head = lax.dot_general(hidden, grads, (((0,), (0,)), ((), ())), preferred_element_type=F32).astype(BF16)
    kept, received, grad_head = lax.optimization_barrier((kept, received, grad_head))
    total = kept + received.astype(F32)
    for stage in (2, 1, 0):
        size = total.shape[0] // 4
        parts = [shift(total[k * size : (k + 1) * size].astype(BF16), stage, -k) for k in (1, 2, 3)]
        total = total[:size] + sum(p.astype(F32) for p in parts)
    token_loss = lax.dynamic_slice_in_dim(loss[0], lax.axis_index(AXES) * ROWS, ROWS)
    return token_loss, grad_head, total.astype(BF16)


def solution(mesh):
    in_specs = (P(AXES, None), P(None, AXES), P(AXES, None), P(None, AXES), P(), P())
    out_specs = (P(AXES), P(None, AXES), P(AXES, None))
    return jax.shard_map(shards, mesh=mesh, in_specs=in_specs, out_specs=out_specs, check_vma=False)
```

```python
import functools
import math

import jax
import jax.numpy as jnp
from jax import lax
from jax.experimental import pallas as pl
from jax.experimental.pallas import tpu as pltpu
from jax.sharding import PartitionSpec as P


AXES = ("grp", "tp")
DEVICES = 128
TOKENS = 384
ROWS = 3
HALF = TOKENS // 2
BF16 = jnp.bfloat16
F32 = jnp.float32
VMEM = pl.BlockSpec(memory_space=pltpu.VMEM)
SMEM = pl.BlockSpec(memory_space=pltpu.SMEM)
HBM = pl.BlockSpec(memory_space=pltpu.HBM)
STAGES = (("y", "x", "z"), ("z", "y", "x"))


def coords(d):
    return {"zl": d // 64, "c": d // 32 % 2, "zh": d // 16 % 2, "x": d // 4 % 4, "y": d % 4, "z": d // 16 % 2 * 2 + d // 64}


def device(c, x, y, z):
    return ((z % 2 * 2 + c) * 2 + z // 2) * 16 + x * 4 + y


def moved(d, dim, k):
    at = coords(d)
    at[dim] = (at[dim] + k) % 4
    return device(at["c"], at["x"], at["y"], at["z"])


def swap(value):
    return lax.ppermute(value, AXES, [(d, d ^ 32) for d in range(DEVICES)])


def shift(value, stage, k):
    pairs = [(d, moved(d, STAGES[coords(d)["c"]][stage], k)) for d in range(DEVICES)]
    return lax.ppermute(value, AXES, pairs)


def token_order(me):
    j = lax.iota(jnp.int32, TOKENS)
    r = j % HALF
    steps = (r // 3 % 4, r // 12 % 4, r // 48)
    tokens = []
    for core in range(2):
        at = {dim: (me[dim] - step) % 4 for dim, step in zip(STAGES[core], steps)}
        tokens.append(device(core, at["x"], at["y"], at["z"]) * ROWS + r % ROWS)
    first = (j < HALF) == (me["c"] == 0)
    return jnp.where(first, tokens[0], tokens[1])[None, :]


def stack(pieces):
    total, at = sum(p.shape[0] for p in pieces), 0
    padded = []
    for p in pieces:
        low = jnp.array(-jnp.inf, p.dtype)
        padded.append(lax.pad(p, low, ((at, total - at - p.shape[0], 0), (0, 0, 0))))
        at += p.shape[0]
    return functools.reduce(jnp.maximum, padded)


def split3(v):
    high = v.astype(BF16)
    rest = v - high.astype(F32)
    middle = rest.astype(BF16)
    return high, middle, (rest - middle.astype(F32)).astype(BF16)


def one_hot(column, row):
    return jnp.where(column == row, 1.0, 0.0).astype(BF16)


def dot(a, b):
    return jnp.dot(a, b, preferred_element_type=F32)


def dot_nt(a, b):
    return lax.dot_general(a, b, (((1,), (1,)), ((), ())), preferred_element_type=F32)


def lane_ids():
    return lax.broadcasted_iota(jnp.int32, (TOKENS, TOKENS), 1)


def to_column(row):
    same = lax.broadcasted_iota(jnp.int32, (TOKENS, TOKENS), 0) == lane_ids()
    return jnp.sum(jnp.where(same, row.astype(F32), 0.0), axis=1, keepdims=True).astype(jnp.int32)


def pick_column(column, row_values):
    return jnp.sum(jnp.where(column == lane_ids(), row_values.astype(F32), 0.0), axis=1, keepdims=True).astype(jnp.int32)


def teacher_kernel(n, *refs):
    blocks, (source, tok_row, owner, w, saved, out, wbuf, sem) = refs[:n], refs[n:]
    slots, chunk, _ = wbuf.shape
    count = w.shape[0] // chunk

    def copy(i):
        slot = i % slots
        return pltpu.make_async_copy(w.at[pl.ds(i * chunk, chunk), :], wbuf.at[slot], sem.at[slot])

    for i in range(slots):
        copy(i).start()
    for i in range(count):
        columns = slice(i * chunk, (i + 1) * chunk)
        rows = jnp.concatenate([block[:, columns] for block in blocks], axis=0)
        copy(i).wait()
        part = dot(rows, wbuf[i % slots])
        out[...] = part if i == 0 else out[...] + part
        if i + slots < count:
            copy(i + slots).start()
    owner_col = pick_column(to_column(tok_row[...]), owner[...])
    pick = one_hot(owner_col, source[...])
    high, middle, low = split3(out[...])
    saves = []
    for i in range(3):
        rows = slice(i * 128, (i + 1) * 128)
        out[rows, :] = (dot(pick[rows], high) + dot(pick[rows], middle)) + dot(pick[rows], low)
        saves.append(pltpu.make_async_copy(out.at[rows, :], saved.at[rows, :], sem.at[slots + i]))
        saves[-1].start()
    for save in saves:
        save.wait()


def student_kernel(n, *refs):
    blocks, refs = refs[:n], refs[n:]
    at_ref, t_in, tok_row, labels, w, s_save, g_save, stats_out, t_ref, s_out, g, wbuf, table, label_at, sem = refs
    chunk = 896
    count = w.shape[0] // chunk

    def copy(i):
        rows = pl.ds(pl.multiple_of(i * chunk, chunk), chunk)
        return pltpu.make_async_copy(w.at[rows, :], wbuf.at[rows, :], sem.at[i])

    for i in range(count):
        copy(i).start()
    at = 0
    for block in blocks:
        g[pl.ds(at, block.shape[0]), :] = block[...]
        at += block.shape[0]
    load = pltpu.make_async_copy(t_in, t_ref, sem.at[count + 2])
    load.start()
    saves = [pltpu.make_async_copy(*pair, sem.at[count + i]) for i, pair in enumerate([(g, g_save), (s_out, s_save)])]
    saves[0].start()
    s_out[...] = jnp.zeros_like(s_out)
    tok_col = to_column(tok_row[...])
    label_at[...] = pick_column(tok_col, labels[...]) - at_ref[0]

    @pl.loop(0, count)
    def _(i):
        rows = pl.ds(pl.multiple_of(i * chunk, chunk), chunk)
        copy(i).wait()
        s_out[...] += dot(g[:, rows], wbuf[rows, :])

    saves[1].start()
    load.wait()
    step = 64
    lane = lax.broadcasted_iota(jnp.int32, (step, 128), 1)
    for i in range(TOKENS // step):
        rows = slice(i * step, (i + 1) * step)
        t = t_ref[rows, :]
        s = s_out[rows, :]
        t_top = jnp.max(t, axis=1, keepdims=True)
        s_top = jnp.max(s, axis=1, keepdims=True)
        t_low, s_low, gap = t - t_top, s - s_top, t - s
        t_exp, s_exp = jnp.exp(t_low), jnp.exp(s_low)
        hits = lax.broadcasted_iota(jnp.int32, t.shape, 1) == label_at[rows, :]
        values = (
            t_top,
            jnp.sum(t_exp, axis=1, keepdims=True),
            jnp.sum(t_exp * t_low, axis=1, keepdims=True),
            jnp.sum(t_exp * gap, axis=1, keepdims=True),
            s_top,
            jnp.sum(s_exp, axis=1, keepdims=True),
            jnp.sum(-s_exp * gap, axis=1, keepdims=True),
            jnp.sum(jnp.where(hits, s, 0.0), axis=1, keepdims=True),
        )
        packed = jnp.zeros((step, 128), F32)
        for k, value in enumerate(values):
            packed = jnp.where(lane == k, value, packed)
        table[rows, :] = packed

    to_natural = one_hot(tok_col, lane_ids())
    high, middle, low = split3(table[...].T[:16])
    stats_out[...] = ((dot(high, to_natural) + dot(middle, to_natural)) + dot(low, to_natural))[:8]
    for save in saves:
        save.wait()


def weight_copies(w, wbuf, sem):
    chunk = 896
    slices = [slice(i * chunk, (i + 1) * chunk) for i in range(w.shape[0] // chunk)]
    copies = [(rows, pltpu.make_async_copy(w.at[rows, :], wbuf.at[rows, :], sem.at[i])) for i, rows in enumerate(slices)]
    for _, copy in copies:
        copy.start()
    return copies


def gradient_kernel(vocab, at_ref, t_in, s_in, stats, tok_row, labels, w, grads_out, send_out, keep_out, loss_out, t_ref, s_ref, wbuf, local, label_at, sem):
    loads = [pltpu.make_async_copy(*pair, sem.at[4 + i]) for i, pair in enumerate([(t_in, t_ref), (s_in, s_ref)])]
    for load in loads:
        load.start()
    copies = weight_copies(w, wbuf, sem)
    t_top, t_sum, t_moment, t_gap, s_top, s_sum, s_gap, hit = (stats[k : k + 1, :] for k in range(8))
    t_log, s_log = jnp.log(t_sum), jnp.log(s_sum)
    t_lse, s_lse = t_top + t_log, s_top + s_log
    weight = (t_log - t_moment / t_sum) / math.log(vocab)
    forward = t_gap / t_sum - t_lse + s_lse
    reverse = s_gap / s_sum - s_lse + t_lse
    loss_out[...] = weight * forward + (1.0 - weight) * reverse + (s_lse - hit)
    rows8 = jnp.concatenate([t_lse, s_lse, weight, reverse] * 2, axis=0)
    tok_col = to_column(tok_row[...])
    from_natural = one_hot(tok_col, lane_ids())
    label_at[...] = pick_column(tok_col, labels[...]) - at_ref[0]
    high, middle, low = split3(rows8)
    local[...] = (dot_nt(from_natural, high) + dot_nt(from_natural, middle)) + dot_nt(from_natural, low)
    for load in loads:
        load.wait()
    step = 64
    for i in range(TOKENS // step):
        rows = slice(i * step, (i + 1) * step)
        t_lse, s_lse, weight, reverse = (local[rows, k : k + 1] for k in range(4))
        t_log = t_ref[rows, :] - t_lse
        s_log = s_ref[rows, :] - s_lse
        t_prob, s_prob = jnp.exp(t_log), jnp.exp(s_log)
        mixed = weight * (s_prob - t_prob) + (1.0 - weight) * s_prob * (s_log - t_log - reverse)
        hits = lax.broadcasted_iota(jnp.int32, t_log.shape, 1) == label_at[rows, :]
        mixed = mixed + s_prob - jnp.where(hits, 1.0, 0.0)
        grads_out[rows, :] = (mixed / TOKENS).astype(BF16)

    for rows, copy in copies:
        copy.wait()
        part = dot_nt(grads_out[...], wbuf[rows, :])
        send_out[:, rows] = part[HALF:].astype(BF16)
        keep_out[:, rows] = part[:HALF]


def call(kernel, out, specs, args, scratch, vmem, flops, out_specs=None):
    return pl.pallas_call(
        kernel,
        out_shape=[jax.ShapeDtypeStruct(*o) for o in out],
        in_specs=specs,
        out_specs=out_specs or [VMEM] * len(out),
        scratch_shapes=scratch,
        compiler_params=pltpu.CompilerParams(vmem_limit_bytes=vmem << 20),
        cost_estimate=pl.CostEstimate(flops=flops, bytes_accessed=4 << 20, transcendentals=0),
    )(*args)


def merge(tables):
    t_top = functools.reduce(jnp.maximum, [v[0] for v in tables])
    s_top = functools.reduce(jnp.maximum, [v[4] for v in tables])
    total = 0.0
    for v in tables:
        t_low, s_low = v[0] - t_top, v[4] - s_top
        t_scale, s_scale = jnp.exp(t_low), jnp.exp(s_low)
        total += jnp.stack(
            [
                jnp.zeros_like(t_top), t_scale * v[1], t_scale * (v[2] + t_low * v[1]), t_scale * v[3],
                jnp.zeros_like(s_top), s_scale * v[5], s_scale * v[6], v[7],
            ]
        )
    row = lax.broadcasted_iota(jnp.int32, total.shape, 0)
    return jnp.where(row == 0, t_top, jnp.where(row == 4, s_top, total))


def ring_shift(value, dim):
    return lax.ppermute(value, AXES, [(d, moved(d, dim, -1 if coords(d)["c"] else 1)) for d in range(DEVICES)])


def across(value, dim):
    return lax.ppermute(value, AXES, [(d, moved(d, dim, 2)) for d in range(DEVICES)])


def shards(teacher_hidden, teacher_head, student_hidden, student_head, labels, owner_map):
    me = coords(lax.axis_index(AXES))
    vocab = teacher_head.shape[1]
    tk, sk = teacher_head.shape[0], student_head.shape[0]
    tok_row = token_order(me)
    at = (lax.axis_index(AXES) * vocab).astype(jnp.int32)[None]
    label_row, owner_row = labels[None, :], owner_map[None, :]

    parts = [teacher_hidden] + [shift(teacher_hidden, 0, k) for k in (1, 2, 3)]
    t = stack(parts)
    t = [t] + [shift(t, 1, k) for k in (1, 2, 3)]
    parts = [student_hidden] + [shift(student_hidden, 0, k) for k in (1, 2, 3)]
    s = stack(parts)
    s = stack([s] + [shift(s, 1, k) for k in (1, 2, 3)])
    a, b = stack(t[:2]), stack(t[2:])
    before_a, after_b = shift(a, 2, 1), shift(b, 2, -1)
    before_b, after_a = shift(b, 2, 1), shift(a, 2, -1)
    far = [shift(before_a, 2, 1), shift(after_b, 2, -1)]
    s_moved = [shift(s, 2, k) for k in (1, 2, 3)]
    near = [before_a, before_b, after_a, after_b]
    near = [a, b, *near, swap(a), swap(b), *[swap(v) for v in near]]
    far = far + [swap(v) for v in far]
    s0 = s

    blocks = near + far
    q = HALF // 4
    pieces = [tok_row[:, at * q : (at + 1) * q] for at in (0, 1, 3, 4, 5, 7, 2, 6)]
    source = jnp.concatenate(pieces, axis=1)
    (t_logits,) = call(
        functools.partial(teacher_kernel, len(blocks)),
        [((TOKENS, vocab), F32)],
        [VMEM] * (len(blocks) + 3) + [HBM],
        [*blocks, source, tok_row, owner_row, teacher_head],
        [pltpu.VMEM((TOKENS, vocab), F32), pltpu.VMEM((3, 1024, vocab), BF16), pltpu.SemaphoreType.DMA((6,))],
        50,
        2 * TOKENS * tk * vocab,
        [HBM],
    )
    *s_moved, t_logits = lax.optimization_barrier((*s_moved, t_logits))
    s_own = [s0, *s_moved]
    s_blocks = s_own + [swap(v) for v in s_own]
    n = len(s_blocks)
    s_logits, hidden, stats = call(
        functools.partial(student_kernel, n),
        [((TOKENS, vocab), F32), ((TOKENS, sk), BF16), ((8, TOKENS), F32)],
        [VMEM] * n + [SMEM, HBM] + [VMEM] * 2 + [HBM],
        [*s_blocks, at, t_logits, tok_row, label_row, student_head],
        [
            pltpu.VMEM((TOKENS, vocab), F32),
            pltpu.VMEM((TOKENS, vocab), F32),
            pltpu.VMEM((TOKENS, sk), BF16),
            pltpu.VMEM((sk, vocab), BF16),
            pltpu.VMEM((TOKENS, 128), F32),
            pltpu.VMEM((TOKENS, 1), jnp.int32),
            pltpu.SemaphoreType.DMA((7,)),
        ],
        50,
        2 * TOKENS * sk * vocab,
        [HBM, HBM, VMEM],
    )

    stats = merge([stats, swap(stats)])
    for dim in ("y", "x", "z"):
        near, far = ring_shift(stats, dim), across(stats, dim)
        stats = merge([stats, near, swap(near), far])

    grads, to_other, kept, loss = call(
        functools.partial(gradient_kernel, vocab * DEVICES),
        [((TOKENS, vocab), BF16), ((HALF, sk), BF16), ((HALF, sk), F32), ((1, TOKENS), F32)],
        [SMEM] + [HBM] * 2 + [VMEM] * 3 + [HBM],
        [at, t_logits, s_logits, stats, tok_row, label_row, student_head],
        [
            pltpu.VMEM((TOKENS, vocab), F32),
            pltpu.VMEM((TOKENS, vocab), F32),
            pltpu.VMEM((sk, vocab), BF16),
            pltpu.VMEM((TOKENS, 8), F32),
            pltpu.VMEM((TOKENS, 1), jnp.int32),
            pltpu.SemaphoreType.DMA((6,)),
        ],
        46,
        2 * TOKENS * sk * vocab,
    )

    received = swap(to_other)
    grad_head = lax.dot_general(hidden, grads, (((0,), (0,)), ((), ())), preferred_element_type=F32).astype(BF16)
    kept, received, grad_head = lax.optimization_barrier((kept, received, grad_head))
    total = kept + received.astype(F32)
    for stage in (2, 1, 0):
        size = total.shape[0] // 4
        parts = [shift(total[k * size : (k + 1) * size].astype(BF16), stage, -k) for k in (1, 2, 3)]
        total = total[:size] + sum(p.astype(F32) for p in parts)
    token_loss = lax.dynamic_slice_in_dim(loss[0], lax.axis_index(AXES) * ROWS, ROWS)
    return token_loss, grad_head, total.astype(BF16)


def solution(mesh):
    in_specs = (P(AXES, None), P(None, AXES), P(AXES, None), P(None, AXES), P(), P())
    out_specs = (P(AXES), P(None, AXES), P(AXES, None))
    return jax.shard_map(shards, mesh=mesh, in_specs=in_specs, out_specs=out_specs, check_vma=False)
```

```python
import functools
import math

import jax
import jax.numpy as jnp
from jax import lax
from jax.experimental import pallas as pl
from jax.experimental.pallas import tpu as pltpu
from jax.sharding import PartitionSpec as P


AXES = ("grp", "tp")
DEVICES = 128
TOKENS = 384
ROWS = 3
HALF = TOKENS // 2
BF16 = jnp.bfloat16
F32 = jnp.float32
VMEM = pl.BlockSpec(memory_space=pltpu.VMEM)
SMEM = pl.BlockSpec(memory_space=pltpu.SMEM)
HBM = pl.BlockSpec(memory_space=pltpu.HBM)
STAGES = (("y", "x", "z"), ("z", "y", "x"))


def coords(d):
    return {"zl": d // 64, "c": d // 32 % 2, "zh": d // 16 % 2, "x": d // 4 % 4, "y": d % 4, "z": d // 16 % 2 * 2 + d // 64}


def device(c, x, y, z):
    return ((z % 2 * 2 + c) * 2 + z // 2) * 16 + x * 4 + y


def moved(d, dim, k):
    at = coords(d)
    at[dim] = (at[dim] + k) % 4
    return device(at["c"], at["x"], at["y"], at["z"])


def swap(value):
    return lax.ppermute(value, AXES, [(d, d ^ 32) for d in range(DEVICES)])


def shift(value, stage, k):
    pairs = [(d, moved(d, STAGES[coords(d)["c"]][stage], k)) for d in range(DEVICES)]
    return lax.ppermute(value, AXES, pairs)


def token_order(me):
    j = lax.iota(jnp.int32, TOKENS)
    r = j % HALF
    steps = (r // 3 % 4, r // 12 % 4, r // 48)
    tokens = []
    for core in range(2):
        at = {dim: (me[dim] - step) % 4 for dim, step in zip(STAGES[core], steps)}
        tokens.append(device(core, at["x"], at["y"], at["z"]) * ROWS + r % ROWS)
    first = (j < HALF) == (me["c"] == 0)
    return jnp.where(first, tokens[0], tokens[1])[None, :]


def stack(pieces):
    total, at = sum(p.shape[0] for p in pieces), 0
    padded = []
    for p in pieces:
        low = jnp.array(-jnp.inf, p.dtype)
        padded.append(lax.pad(p, low, ((at, total - at - p.shape[0], 0), (0, 0, 0))))
        at += p.shape[0]
    return functools.reduce(jnp.maximum, padded)


def split3(v):
    high = v.astype(BF16)
    rest = v - high.astype(F32)
    middle = rest.astype(BF16)
    return high, middle, (rest - middle.astype(F32)).astype(BF16)


def one_hot(column, row):
    return jnp.where(column == row, 1.0, 0.0).astype(BF16)


def dot(a, b):
    return jnp.dot(a, b, preferred_element_type=F32)


def dot_nt(a, b):
    return lax.dot_general(a, b, (((1,), (1,)), ((), ())), preferred_element_type=F32)


def lane_ids():
    return lax.broadcasted_iota(jnp.int32, (TOKENS, TOKENS), 1)


def to_column(row):
    same = lax.broadcasted_iota(jnp.int32, (TOKENS, TOKENS), 0) == lane_ids()
    return jnp.sum(jnp.where(same, row.astype(F32), 0.0), axis=1, keepdims=True).astype(jnp.int32)


def pick_column(column, row_values):
    return jnp.sum(jnp.where(column == lane_ids(), row_values.astype(F32), 0.0), axis=1, keepdims=True).astype(jnp.int32)


def teacher_kernel(n, fetched, *refs):
    blocks, (source, tok_row, owner, w, saved, out, wbuf, gbuf, sem, gsem) = list(refs[:n]), refs[n:]
    fetches = [pltpu.make_async_copy(blocks[at], gbuf.at[i], gsem.at[i]) for i, at in enumerate(fetched)]
    for fetch in fetches:
        fetch.start()
    slots, chunk, _ = wbuf.shape
    count = w.shape[0] // chunk

    def copy(i):
        slot = i % slots
        return pltpu.make_async_copy(w.at[pl.ds(i * chunk, chunk), :], wbuf.at[slot], sem.at[slot])

    for i in range(slots):
        copy(i).start()
    owner_col = pick_column(to_column(tok_row[...]), owner[...])
    pick = one_hot(owner_col, source[...])
    for i, at in enumerate(fetched):
        fetches[i].wait()
        blocks[at] = gbuf.at[i]
    for i in range(count):
        columns = slice(i * chunk, (i + 1) * chunk)
        rows = jnp.concatenate([block[:, columns] for block in blocks], axis=0)
        copy(i).wait()
        part = dot(rows, wbuf[i % slots])
        out[...] = part if i == 0 else out[...] + part
        if i + slots < count:
            copy(i + slots).start()
    high, middle, low = split3(out[...])
    saves = []
    for i in range(3):
        rows = slice(i * 128, (i + 1) * 128)
        out[rows, :] = (dot(pick[rows], high) + dot(pick[rows], middle)) + dot(pick[rows], low)
        saves.append(pltpu.make_async_copy(out.at[rows, :], saved.at[rows, :], sem.at[slots + i]))
        saves[-1].start()
    for save in saves:
        save.wait()


def student_kernel(n, *refs):
    blocks, refs = refs[:n], refs[n:]
    at_ref, t_in, tok_row, labels, w, s_save, g_save, stats_out, t_ref, s_out, g, wbuf, table, label_at, sem = refs
    chunk = 896
    count = w.shape[0] // chunk

    def copy(i):
        rows = pl.ds(pl.multiple_of(i * chunk, chunk), chunk)
        return pltpu.make_async_copy(w.at[rows, :], wbuf.at[rows, :], sem.at[i])

    for i in range(count):
        copy(i).start()
    at = 0
    for block in blocks:
        g[pl.ds(at, block.shape[0]), :] = block[...]
        at += block.shape[0]
    load = pltpu.make_async_copy(t_in, t_ref, sem.at[count + 2])
    load.start()
    saves = [pltpu.make_async_copy(*pair, sem.at[count + i]) for i, pair in enumerate([(g, g_save), (s_out, s_save)])]
    saves[0].start()
    s_out[...] = jnp.zeros_like(s_out)
    tok_col = to_column(tok_row[...])
    label_at[...] = pick_column(tok_col, labels[...]) - at_ref[0]
    to_natural = one_hot(tok_col, lane_ids())

    @pl.loop(0, count)
    def _(i):
        rows = pl.ds(pl.multiple_of(i * chunk, chunk), chunk)
        copy(i).wait()
        s_out[...] += dot(g[:, rows], wbuf[rows, :])

    saves[1].start()
    load.wait()
    step = 64
    lane = lax.broadcasted_iota(jnp.int32, (step, 128), 1)
    for i in range(TOKENS // step):
        rows = slice(i * step, (i + 1) * step)
        t = t_ref[rows, :]
        s = s_out[rows, :]
        t_top = jnp.max(t, axis=1, keepdims=True)
        s_top = jnp.max(s, axis=1, keepdims=True)
        t_low, s_low, gap = t - t_top, s - s_top, t - s
        t_exp, s_exp = jnp.exp(t_low), jnp.exp(s_low)
        hits = lax.broadcasted_iota(jnp.int32, t.shape, 1) == label_at[rows, :]
        values = (
            t_top,
            jnp.sum(t_exp, axis=1, keepdims=True),
            jnp.sum(t_exp * t_low, axis=1, keepdims=True),
            jnp.sum(t_exp * gap, axis=1, keepdims=True),
            s_top,
            jnp.sum(s_exp, axis=1, keepdims=True),
            jnp.sum(-s_exp * gap, axis=1, keepdims=True),
            jnp.sum(jnp.where(hits, s, 0.0), axis=1, keepdims=True),
        )
        packed = jnp.zeros((step, 128), F32)
        for k, value in enumerate(values):
            packed = jnp.where(lane == k, value, packed)
        table[rows, :] = packed

    high, middle, low = split3(table[...].T[:16])
    stats_out[...] = ((dot(high, to_natural) + dot(middle, to_natural)) + dot(low, to_natural))[:8]
    for save in saves:
        save.wait()


def weight_copies(w, wbuf, sem):
    chunk = 896
    slices = [slice(i * chunk, (i + 1) * chunk) for i in range(w.shape[0] // chunk)]
    copies = [(rows, pltpu.make_async_copy(w.at[rows, :], wbuf.at[rows, :], sem.at[i])) for i, rows in enumerate(slices)]
    for _, copy in copies:
        copy.start()
    return copies


def gradient_kernel(vocab, at_ref, t_in, s_in, stats, tok_row, labels, w, grads_out, send_out, keep_out, loss_out, t_ref, s_ref, wbuf, local, label_at, sem):
    loads = [pltpu.make_async_copy(*pair, sem.at[4 + i]) for i, pair in enumerate([(t_in, t_ref), (s_in, s_ref)])]
    for load in loads:
        load.start()
    copies = weight_copies(w, wbuf, sem)
    t_top, t_sum, t_moment, t_gap, s_top, s_sum, s_gap, hit = (stats[k : k + 1, :] for k in range(8))
    t_log, s_log = jnp.log(t_sum), jnp.log(s_sum)
    t_lse, s_lse = t_top + t_log, s_top + s_log
    weight = (t_log - t_moment / t_sum) / math.log(vocab)
    forward = t_gap / t_sum - t_lse + s_lse
    reverse = s_gap / s_sum - s_lse + t_lse
    loss_out[...] = weight * forward + (1.0 - weight) * reverse + (s_lse - hit)
    rows8 = jnp.concatenate([t_lse, s_lse, weight, reverse] * 2, axis=0)
    tok_col = to_column(tok_row[...])
    from_natural = one_hot(tok_col, lane_ids())
    label_at[...] = pick_column(tok_col, labels[...]) - at_ref[0]
    high, middle, low = split3(rows8)
    local[...] = (dot_nt(from_natural, high) + dot_nt(from_natural, middle)) + dot_nt(from_natural, low)
    for load in loads:
        load.wait()
    step = 64
    for i in range(TOKENS // step):
        rows = slice(i * step, (i + 1) * step)
        t_lse, s_lse, weight, reverse = (local[rows, k : k + 1] for k in range(4))
        t_log = t_ref[rows, :] - t_lse
        s_log = s_ref[rows, :] - s_lse
        t_prob, s_prob = jnp.exp(t_log), jnp.exp(s_log)
        mixed = weight * (s_prob - t_prob) + (1.0 - weight) * s_prob * (s_log - t_log - reverse)
        hits = lax.broadcasted_iota(jnp.int32, t_log.shape, 1) == label_at[rows, :]
        mixed = mixed + s_prob - jnp.where(hits, 1.0, 0.0)
        grads_out[rows, :] = (mixed / TOKENS).astype(BF16)

    for rows, copy in copies:
        copy.wait()
        part = dot_nt(grads_out[...], wbuf[rows, :])
        send_out[:, rows] = part[HALF:].astype(BF16)
        keep_out[:, rows] = part[:HALF]


def call(kernel, out, specs, args, scratch, vmem, flops, out_specs=None):
    return pl.pallas_call(
        kernel,
        out_shape=[jax.ShapeDtypeStruct(*o) for o in out],
        in_specs=specs,
        out_specs=out_specs or [VMEM] * len(out),
        scratch_shapes=scratch,
        compiler_params=pltpu.CompilerParams(vmem_limit_bytes=vmem << 20),
        cost_estimate=pl.CostEstimate(flops=flops, bytes_accessed=4 << 20, transcendentals=0),
    )(*args)


def merge(tables):
    t_top = functools.reduce(jnp.maximum, [v[0] for v in tables])
    s_top = functools.reduce(jnp.maximum, [v[4] for v in tables])
    total = 0.0
    for v in tables:
        t_low, s_low = v[0] - t_top, v[4] - s_top
        t_scale, s_scale = jnp.exp(t_low), jnp.exp(s_low)
        total += jnp.stack(
            [
                jnp.zeros_like(t_top), t_scale * v[1], t_scale * (v[2] + t_low * v[1]), t_scale * v[3],
                jnp.zeros_like(s_top), s_scale * v[5], s_scale * v[6], v[7],
            ]
        )
    row = lax.broadcasted_iota(jnp.int32, total.shape, 0)
    return jnp.where(row == 0, t_top, jnp.where(row == 4, s_top, total))


def ring_shift(value, dim):
    return lax.ppermute(value, AXES, [(d, moved(d, dim, -1 if coords(d)["c"] else 1)) for d in range(DEVICES)])


def across(value, dim):
    return lax.ppermute(value, AXES, [(d, moved(d, dim, 2)) for d in range(DEVICES)])


def shards(teacher_hidden, teacher_head, student_hidden, student_head, labels, owner_map):
    me = coords(lax.axis_index(AXES))
    vocab = teacher_head.shape[1]
    tk, sk = teacher_head.shape[0], student_head.shape[0]
    tok_row = token_order(me)
    at = (lax.axis_index(AXES) * vocab).astype(jnp.int32)[None]
    label_row, owner_row = labels[None, :], owner_map[None, :]

    parts = [teacher_hidden] + [shift(teacher_hidden, 0, k) for k in (1, 2, 3)]
    t = stack(parts)
    t = [t] + [shift(t, 1, k) for k in (1, 2, 3)]
    parts = [student_hidden] + [shift(student_hidden, 0, k) for k in (1, 2, 3)]
    s = stack(parts)
    s = stack([s] + [shift(s, 1, k) for k in (1, 2, 3)])
    a, b = stack(t[:2]), stack(t[2:])
    before_a, after_b = shift(a, 2, 1), shift(b, 2, -1)
    before_b, after_a = shift(b, 2, 1), shift(a, 2, -1)
    far = [shift(before_a, 2, 1), shift(after_b, 2, -1)]
    s_moved = [shift(s, 2, k) for k in (1, 2, 3)]
    near = [before_a, before_b, after_a, after_b]
    near = [a, b, *near, swap(a), swap(b), *[swap(v) for v in near]]
    far = far + [swap(v) for v in far]
    s0 = s

    blocks = near + far
    fetched = (6, 7, 8, 9, 10, 11, 14, 15)
    q = HALF // 4
    pieces = [tok_row[:, at * q : (at + 1) * q] for at in (0, 1, 3, 4, 5, 7, 2, 6)]
    source = jnp.concatenate(pieces, axis=1)
    (t_logits,) = call(
        functools.partial(teacher_kernel, len(blocks), fetched),
        [((TOKENS, vocab), F32)],
        [HBM if i in fetched else VMEM for i in range(len(blocks))] + [VMEM] * 3 + [HBM],
        [*blocks, source, tok_row, owner_row, teacher_head],
        [
            pltpu.VMEM((TOKENS, vocab), F32),
            pltpu.VMEM((3, 1024, vocab), BF16),
            pltpu.VMEM((len(fetched), *blocks[0].shape), BF16),
            pltpu.SemaphoreType.DMA((6,)),
            pltpu.SemaphoreType.DMA((len(fetched),)),
        ],
        47,
        2 * TOKENS * tk * vocab,
        [HBM],
    )
    *s_moved, t_logits = lax.optimization_barrier((*s_moved, t_logits))
    s_own = [s0, *s_moved]
    s_blocks = s_own + [swap(v) for v in s_own]
    n = len(s_blocks)
    s_logits, hidden, stats = call(
        functools.partial(student_kernel, n),
        [((TOKENS, vocab), F32), ((TOKENS, sk), BF16), ((8, TOKENS), F32)],
        [VMEM] * n + [SMEM, HBM] + [VMEM] * 2 + [HBM],
        [*s_blocks, at, t_logits, tok_row, label_row, student_head],
        [
            pltpu.VMEM((TOKENS, vocab), F32),
            pltpu.VMEM((TOKENS, vocab), F32),
            pltpu.VMEM((TOKENS, sk), BF16),
            pltpu.VMEM((sk, vocab), BF16),
            pltpu.VMEM((TOKENS, 128), F32),
            pltpu.VMEM((TOKENS, 1), jnp.int32),
            pltpu.SemaphoreType.DMA((7,)),
        ],
        51,
        2 * TOKENS * sk * vocab,
        [HBM, HBM, VMEM],
    )

    stats = merge([stats, swap(stats)])
    for dim in ("y", "x", "z"):
        near, far = ring_shift(stats, dim), across(stats, dim)
        stats = merge([stats, near, swap(near), far])

    grads, to_other, kept, loss = call(
        functools.partial(gradient_kernel, vocab * DEVICES),
        [((TOKENS, vocab), BF16), ((HALF, sk), BF16), ((HALF, sk), F32), ((1, TOKENS), F32)],
        [SMEM] + [HBM] * 2 + [VMEM] * 3 + [HBM],
        [at, t_logits, s_logits, stats, tok_row, label_row, student_head],
        [
            pltpu.VMEM((TOKENS, vocab), F32),
            pltpu.VMEM((TOKENS, vocab), F32),
            pltpu.VMEM((sk, vocab), BF16),
            pltpu.VMEM((TOKENS, 8), F32),
            pltpu.VMEM((TOKENS, 1), jnp.int32),
            pltpu.SemaphoreType.DMA((6,)),
        ],
        44,
        2 * TOKENS * sk * vocab,
    )

    received = swap(to_other)
    grad_head = lax.dot_general(hidden, grads, (((0,), (0,)), ((), ())), preferred_element_type=F32).astype(BF16)
    total = kept + received.astype(F32)
    for stage in (2, 1, 0):
        size = total.shape[0] // 4
        parts = [shift(total[k * size : (k + 1) * size].astype(BF16), stage, -k) for k in (1, 2, 3)]
        if stage == 2:
            total, grad_head, *parts = lax.optimization_barrier((total, grad_head, *parts))
        total = total[:size] + sum(p.astype(F32) for p in parts)
    token_loss = lax.dynamic_slice_in_dim(loss[0], lax.axis_index(AXES) * ROWS, ROWS)
    return token_loss, grad_head, total.astype(BF16)


def solution(mesh):
    in_specs = (P(AXES, None), P(None, AXES), P(AXES, None), P(None, AXES), P(), P())
    out_specs = (P(AXES), P(None, AXES), P(AXES, None))
    return jax.shard_map(shards, mesh=mesh, in_specs=in_specs, out_specs=out_specs, check_vma=False)
```

```python
import functools
import math

import jax
import jax.numpy as jnp
from jax import lax
from jax.experimental import pallas as pl
from jax.experimental.pallas import tpu as pltpu
from jax.sharding import PartitionSpec as P


AXES = ("grp", "tp")
DEVICES = 128
TOKENS = 384
ROWS = 3
HALF = TOKENS // 2
BF16 = jnp.bfloat16
F32 = jnp.float32
VMEM = pl.BlockSpec(memory_space=pltpu.VMEM)
SMEM = pl.BlockSpec(memory_space=pltpu.SMEM)
HBM = pl.BlockSpec(memory_space=pltpu.HBM)
STAGES = (("y", "x", "z"), ("z", "y", "x"))


def coords(d):
    return {"zl": d // 64, "c": d // 32 % 2, "zh": d // 16 % 2, "x": d // 4 % 4, "y": d % 4, "z": d // 16 % 2 * 2 + d // 64}


def device(c, x, y, z):
    return ((z % 2 * 2 + c) * 2 + z // 2) * 16 + x * 4 + y


def moved(d, dim, k):
    at = coords(d)
    at[dim] = (at[dim] + k) % 4
    return device(at["c"], at["x"], at["y"], at["z"])


def swap(value):
    return lax.ppermute(value, AXES, [(d, d ^ 32) for d in range(DEVICES)])


def shift(value, stage, k):
    pairs = [(d, moved(d, STAGES[coords(d)["c"]][stage], k)) for d in range(DEVICES)]
    return lax.ppermute(value, AXES, pairs)


def token_order(me):
    j = lax.iota(jnp.int32, TOKENS)
    r = j % HALF
    steps = (r // 3 % 4, r // 12 % 4, r // 48)
    tokens = []
    for core in range(2):
        at = {dim: (me[dim] - step) % 4 for dim, step in zip(STAGES[core], steps)}
        tokens.append(device(core, at["x"], at["y"], at["z"]) * ROWS + r % ROWS)
    first = (j < HALF) == (me["c"] == 0)
    return jnp.where(first, tokens[0], tokens[1])[None, :]


def stack(pieces):
    total, at = sum(p.shape[0] for p in pieces), 0
    padded = []
    for p in pieces:
        low = jnp.array(-jnp.inf, p.dtype)
        padded.append(lax.pad(p, low, ((at, total - at - p.shape[0], 0), (0, 0, 0))))
        at += p.shape[0]
    return functools.reduce(jnp.maximum, padded)


def split3(v):
    high = v.astype(BF16)
    rest = v - high.astype(F32)
    middle = rest.astype(BF16)
    return high, middle, (rest - middle.astype(F32)).astype(BF16)


def one_hot(column, row):
    return jnp.where(column == row, 1.0, 0.0).astype(BF16)


def dot(a, b):
    return jnp.dot(a, b, preferred_element_type=F32)


def dot_nt(a, b):
    return lax.dot_general(a, b, (((1,), (1,)), ((), ())), preferred_element_type=F32)


def lane_ids():
    return lax.broadcasted_iota(jnp.int32, (TOKENS, TOKENS), 1)


def to_column(row):
    same = lax.broadcasted_iota(jnp.int32, (TOKENS, TOKENS), 0) == lane_ids()
    return jnp.sum(jnp.where(same, row.astype(F32), 0.0), axis=1, keepdims=True).astype(jnp.int32)


def pick_column(column, row_values):
    return jnp.sum(jnp.where(column == lane_ids(), row_values.astype(F32), 0.0), axis=1, keepdims=True).astype(jnp.int32)


def teacher_kernel(n, *refs):
    blocks, (source, tok_row, owner, w, saved, out, wbuf, sem) = refs[:n], refs[n:]
    slots, chunk, _ = wbuf.shape
    count = w.shape[0] // chunk

    def copy(i):
        slot = i % slots
        return pltpu.make_async_copy(w.at[pl.ds(i * chunk, chunk), :], wbuf.at[slot], sem.at[slot])

    for i in range(slots):
        copy(i).start()
    for i in range(count):
        columns = slice(i * chunk, (i + 1) * chunk)
        rows = jnp.concatenate([block[:, columns] for block in blocks], axis=0)
        copy(i).wait()
        part = dot(rows, wbuf[i % slots])
        out[...] = part if i == 0 else out[...] + part
        if i + slots < count:
            copy(i + slots).start()
    owner_col = pick_column(to_column(tok_row[...]), owner[...])
    pick = one_hot(owner_col, source[...])
    high, middle, low = split3(out[...])
    saves = []
    for i in range(3):
        rows = slice(i * 128, (i + 1) * 128)
        out[rows, :] = (dot(pick[rows], high) + dot(pick[rows], middle)) + dot(pick[rows], low)
        saves.append(pltpu.make_async_copy(out.at[rows, :], saved.at[rows, :], sem.at[slots + i]))
        saves[-1].start()
    for save in saves:
        save.wait()


def student_kernel(n, *refs):
    blocks, refs = refs[:n], refs[n:]
    at_ref, t_in, tok_row, labels, w, s_save, g_save, stats_out, t_ref, s_out, g, wbuf, table, label_at, sem = refs
    chunk = 896
    count = w.shape[0] // chunk

    def copy(i):
        rows = pl.ds(pl.multiple_of(i * chunk, chunk), chunk)
        return pltpu.make_async_copy(w.at[rows, :], wbuf.at[rows, :], sem.at[i])

    for i in range(count):
        copy(i).start()
    at = 0
    for block in blocks:
        g[pl.ds(at, block.shape[0]), :] = block[...]
        at += block.shape[0]
    load = pltpu.make_async_copy(t_in, t_ref, sem.at[count + 2])
    load.start()
    saves = [pltpu.make_async_copy(*pair, sem.at[count + i]) for i, pair in enumerate([(g, g_save), (s_out, s_save)])]
    saves[0].start()
    s_out[...] = jnp.zeros_like(s_out)
    tok_col = to_column(tok_row[...])
    label_at[...] = pick_column(tok_col, labels[...]) - at_ref[0]

    @pl.loop(0, count)
    def _(i):
        rows = pl.ds(pl.multiple_of(i * chunk, chunk), chunk)
        copy(i).wait()
        s_out[...] += dot(g[:, rows], wbuf[rows, :])

    saves[1].start()
    load.wait()
    step = 64
    lane = lax.broadcasted_iota(jnp.int32, (step, 128), 1)
    for i in range(TOKENS // step):
        rows = slice(i * step, (i + 1) * step)
        t = t_ref[rows, :]
        s = s_out[rows, :]
        t_top = jnp.max(t, axis=1, keepdims=True)
        s_top = jnp.max(s, axis=1, keepdims=True)
        t_low, s_low, gap = t - t_top, s - s_top, t - s
        t_exp, s_exp = jnp.exp(t_low), jnp.exp(s_low)
        hits = lax.broadcasted_iota(jnp.int32, t.shape, 1) == label_at[rows, :]
        values = (
            t_top,
            jnp.sum(t_exp, axis=1, keepdims=True),
            jnp.sum(t_exp * t_low, axis=1, keepdims=True),
            jnp.sum(t_exp * gap, axis=1, keepdims=True),
            s_top,
            jnp.sum(s_exp, axis=1, keepdims=True),
            jnp.sum(-s_exp * gap, axis=1, keepdims=True),
            jnp.sum(jnp.where(hits, s, 0.0), axis=1, keepdims=True),
        )
        packed = jnp.zeros((step, 128), F32)
        for k, value in enumerate(values):
            packed = jnp.where(lane == k, value, packed)
        table[rows, :] = packed

    to_natural = one_hot(tok_col, lane_ids())
    high, middle, low = split3(table[...].T[:16])
    stats_out[...] = ((dot(high, to_natural) + dot(middle, to_natural)) + dot(low, to_natural))[:8]
    for save in saves:
        save.wait()


def weight_copies(w, wbuf, sem):
    chunk = 896
    slices = [slice(i * chunk, (i + 1) * chunk) for i in range(w.shape[0] // chunk)]
    copies = [(rows, pltpu.make_async_copy(w.at[rows, :], wbuf.at[rows, :], sem.at[i])) for i, rows in enumerate(slices)]
    for _, copy in copies:
        copy.start()
    return copies


def gradient_kernel(vocab, at_ref, t_in, s_in, stats, tok_row, labels, w, grads_out, send_out, keep_out, loss_out, t_ref, s_ref, wbuf, local, label_at, sem):
    loads = [pltpu.make_async_copy(*pair, sem.at[4 + i]) for i, pair in enumerate([(t_in, t_ref), (s_in, s_ref)])]
    for load in loads:
        load.start()
    copies = weight_copies(w, wbuf, sem)
    t_top, t_sum, t_moment, t_gap, s_top, s_sum, s_gap, hit = (stats[k : k + 1, :] for k in range(8))
    t_log, s_log = jnp.log(t_sum), jnp.log(s_sum)
    t_lse, s_lse = t_top + t_log, s_top + s_log
    weight = (t_log - t_moment / t_sum) / math.log(vocab)
    forward = t_gap / t_sum - t_lse + s_lse
    reverse = s_gap / s_sum - s_lse + t_lse
    loss_out[...] = weight * forward + (1.0 - weight) * reverse + (s_lse - hit)
    rows8 = jnp.concatenate([t_lse, s_lse, weight, reverse] * 2, axis=0)
    tok_col = to_column(tok_row[...])
    from_natural = one_hot(tok_col, lane_ids())
    label_at[...] = pick_column(tok_col, labels[...]) - at_ref[0]
    high, middle, low = split3(rows8)
    local[...] = (dot_nt(from_natural, high) + dot_nt(from_natural, middle)) + dot_nt(from_natural, low)
    for load in loads:
        load.wait()
    step = 64
    for i in range(TOKENS // step):
        rows = slice(i * step, (i + 1) * step)
        t_lse, s_lse, weight, reverse = (local[rows, k : k + 1] for k in range(4))
        t_log = t_ref[rows, :] - t_lse
        s_log = s_ref[rows, :] - s_lse
        t_prob, s_prob = jnp.exp(t_log), jnp.exp(s_log)
        mixed = weight * (s_prob - t_prob) + (1.0 - weight) * s_prob * (s_log - t_log - reverse)
        hits = lax.broadcasted_iota(jnp.int32, t_log.shape, 1) == label_at[rows, :]
        mixed = mixed + s_prob - jnp.where(hits, 1.0, 0.0)
        grads_out[rows, :] = (mixed / TOKENS).astype(BF16)

    for rows, copy in copies:
        copy.wait()
        part = dot_nt(grads_out[...], wbuf[rows, :])
        send_out[:, rows] = part[HALF:].astype(BF16)
        keep_out[:, rows] = part[:HALF]


def call(kernel, out, specs, args, scratch, vmem, flops, out_specs=None):
    return pl.pallas_call(
        kernel,
        out_shape=[jax.ShapeDtypeStruct(*o) for o in out],
        in_specs=specs,
        out_specs=out_specs or [VMEM] * len(out),
        scratch_shapes=scratch,
        compiler_params=pltpu.CompilerParams(vmem_limit_bytes=vmem << 20),
        cost_estimate=pl.CostEstimate(flops=flops, bytes_accessed=4 << 20, transcendentals=0),
    )(*args)


def merge(tables):
    t_top = functools.reduce(jnp.maximum, [v[0] for v in tables])
    s_top = functools.reduce(jnp.maximum, [v[4] for v in tables])
    total = 0.0
    for v in tables:
        t_low, s_low = v[0] - t_top, v[4] - s_top
        t_scale, s_scale = jnp.exp(t_low), jnp.exp(s_low)
        total += jnp.stack(
            [
                jnp.zeros_like(t_top), t_scale * v[1], t_scale * (v[2] + t_low * v[1]), t_scale * v[3],
                jnp.zeros_like(s_top), s_scale * v[5], s_scale * v[6], v[7],
            ]
        )
    row = lax.broadcasted_iota(jnp.int32, total.shape, 0)
    return jnp.where(row == 0, t_top, jnp.where(row == 4, s_top, total))


def ring_shift(value, dim):
    return lax.ppermute(value, AXES, [(d, moved(d, dim, -1 if coords(d)["c"] else 1)) for d in range(DEVICES)])


def across(value, dim):
    return lax.ppermute(value, AXES, [(d, moved(d, dim, 2)) for d in range(DEVICES)])


def shards(teacher_hidden, teacher_head, student_hidden, student_head, labels, owner_map):
    me = coords(lax.axis_index(AXES))
    vocab = teacher_head.shape[1]
    tk, sk = teacher_head.shape[0], student_head.shape[0]
    tok_row = token_order(me)
    at = (lax.axis_index(AXES) * vocab).astype(jnp.int32)[None]
    label_row, owner_row = labels[None, :], owner_map[None, :]

    parts = [teacher_hidden] + [shift(teacher_hidden, 0, k) for k in (1, 2, 3)]
    t = stack(parts)
    t = [t] + [shift(t, 1, k) for k in (1, 2, 3)]
    parts = [student_hidden] + [shift(student_hidden, 0, k) for k in (1, 2, 3)]
    s = stack(parts)
    s = stack([s] + [shift(s, 1, k) for k in (1, 2, 3)])
    a, b = stack(t[:2]), stack(t[2:])
    before_a, after_b = shift(a, 2, 1), shift(b, 2, -1)
    before_b, after_a = shift(b, 2, 1), shift(a, 2, -1)
    far = [shift(before_a, 2, 1), shift(after_b, 2, -1)]
    s_moved = [shift(s, 2, k) for k in (1, 2, 3)]
    near = [before_a, before_b, after_a, after_b]
    near = [a, b, *near, swap(a), swap(b), *[swap(v) for v in near]]
    far = far + [swap(v) for v in far]
    s0 = s

    blocks = near + far
    q = HALF // 4
    pieces = [tok_row[:, at * q : (at + 1) * q] for at in (0, 1, 3, 4, 5, 7, 2, 6)]
    source = jnp.concatenate(pieces, axis=1)
    (t_logits,) = call(
        functools.partial(teacher_kernel, len(blocks)),
        [((TOKENS, vocab), F32)],
        [VMEM] * (len(blocks) + 3) + [HBM],
        [*blocks, source, tok_row, owner_row, teacher_head],
        [pltpu.VMEM((TOKENS, vocab), F32), pltpu.VMEM((3, 1024, vocab), BF16), pltpu.SemaphoreType.DMA((6,))],
        47,
        2 * TOKENS * tk * vocab,
        [HBM],
    )
    *s_moved, t_logits = lax.optimization_barrier((*s_moved, t_logits))
    s_own = [s0, *s_moved]
    s_blocks = s_own + [swap(v) for v in s_own]
    n = len(s_blocks)
    s_logits, hidden, stats = call(
        functools.partial(student_kernel, n),
        [((TOKENS, vocab), F32), ((TOKENS, sk), BF16), ((8, TOKENS), F32)],
        [VMEM] * n + [SMEM, HBM] + [VMEM] * 2 + [HBM],
        [*s_blocks, at, t_logits, tok_row, label_row, student_head],
        [
            pltpu.VMEM((TOKENS, vocab), F32),
            pltpu.VMEM((TOKENS, vocab), F32),
            pltpu.VMEM((TOKENS, sk), BF16),
            pltpu.VMEM((sk, vocab), BF16),
            pltpu.VMEM((TOKENS, 128), F32),
            pltpu.VMEM((TOKENS, 1), jnp.int32),
            pltpu.SemaphoreType.DMA((7,)),
        ],
        51,
        2 * TOKENS * sk * vocab,
        [HBM, HBM, VMEM],
    )

    stats = merge([stats, swap(stats)])
    for dim in ("y", "x", "z"):
        near, far = ring_shift(stats, dim), across(stats, dim)
        stats = merge([stats, near, swap(near), far])

    grads, to_other, kept, loss = call(
        functools.partial(gradient_kernel, vocab * DEVICES),
        [((TOKENS, vocab), BF16), ((HALF, sk), BF16), ((HALF, sk), F32), ((1, TOKENS), F32)],
        [SMEM] + [HBM] * 2 + [VMEM] * 3 + [HBM],
        [at, t_logits, s_logits, stats, tok_row, label_row, student_head],
        [
            pltpu.VMEM((TOKENS, vocab), F32),
            pltpu.VMEM((TOKENS, vocab), F32),
            pltpu.VMEM((sk, vocab), BF16),
            pltpu.VMEM((TOKENS, 8), F32),
            pltpu.VMEM((TOKENS, 1), jnp.int32),
            pltpu.SemaphoreType.DMA((6,)),
        ],
        44,
        2 * TOKENS * sk * vocab,
    )

    received = swap(to_other)
    grad_head = lax.dot_general(hidden, grads, (((0,), (0,)), ((), ())), preferred_element_type=F32).astype(BF16)
    total = kept + received.astype(F32)
    for stage in (2, 1, 0):
        size = total.shape[0] // 4
        pieces = [total[k * size : (k + 1) * size].astype(BF16) for k in range(4)]
        parts = [shift(pieces[k], stage, -k) for k in (1, 3)]
        parts.insert(1, shift(pieces[2], stage, -2))
        if stage == 2:
            total, grad_head, *parts = lax.optimization_barrier((total, grad_head, *parts))
        total = total[:size] + sum(p.astype(F32) for p in parts)
    token_loss = lax.dynamic_slice_in_dim(loss[0], lax.axis_index(AXES) * ROWS, ROWS)
    return token_loss, grad_head, total.astype(BF16)


def solution(mesh):
    in_specs = (P(AXES, None), P(None, AXES), P(AXES, None), P(None, AXES), P(), P())
    out_specs = (P(AXES), P(None, AXES), P(AXES, None))
    return jax.shard_map(shards, mesh=mesh, in_specs=in_specs, out_specs=out_specs, check_vma=False)
```
